256 devices in a mesh: nest: 2 (over core), bin: 128 (over y, z, x).
Axes of the slice: x: 4, y: 4, z: 8, core: 2. Of those that a mesh axis runs over, the one named last changes fastest.
Arguments:
- spectra: float32 [2, 1152, 8192], P('nest', 'bin'), may hold values from 0.05 to 2
- courant: float32 [2, 1152], P(None, 'bin'), may hold values from -0.9 to 0.9
- coupling: bfloat16 [1152, 1152], replicated, may hold values from -0.1875 to 0.1875
- growth: float32 [1152], replicated, may hold values from 0.05 to 0.5
- dissipation: float32 [1152], replicated, may hold values from 0.2 to 2
- wind: float32 [2, 8192], P('nest'), may hold values from 0.5 to 2
- neighbours: int32 [2, 4, 8192], P('nest'), may hold values from 0 to 8191, as said below
- wet_mask: int32 [2, 8192], P('nest'), may hold values from 0 to 1, as said below
- send_list: int32 [2, 2048], P('nest'), may hold values from 0 to 8191, as said below
- recv_list: int32 [2, 2048], P('nest'), may hold values from 0 to 8191, as said below
- substep_count: int32 [2], P('nest'), may hold values from 1 to 2, as said below
Outputs:
- new_spectra: float32 [2, 1152, 8192], P('nest', 'bin')
The draws below stay inside these ranges and needn't reach their ends.
Inputs may be any that keep to these rules, and one draw needn't show every extreme that they name: `neighbours`: row 0 holds each point's east neighbour, row 1 west, row 2 north, row 3 south, on a periodic grid of 32 rows of 256 points; grid row r holds the point numbers r * 256 to (r + 1) * 256 - 1 in some order. `wet_mask`: exactly 4096 points of each nest are sea points. `send_list`: distinct sea points of the nest, none of them in recv_list of the same nest. `recv_list`: distinct sea points of the nest. `substep_count`: some nest takes 2 substeps.
All inputs are finite; a program needn't handle non-finite values.
Results may differ from the reference program's by a relative error of at most 0.0012.
Values sent between devices are 32-bit elements; how exact they have to be, the bound alone decides.
A program may use at most 64 MiB of HBM per device.

```python
import math
import jax
import jax.numpy as jnp
from jax import lax

K = 1152
SUBSTEPS = 2
SRC = 5
NESTS = 2
POINTS = 8192
GX = 256
GY = 32
WET = 4096
NB = 2048


def geometry(key, nest_id):
    base_key = jax.random.fold_in(jax.random.fold_in(key, 1237), nest_id)
    key_rows, key_level, key_cols, key_noise, key_pick = jax.random.split(base_key, 5)
    row_keys = jax.random.split(key_rows, GY)
    perms = jax.vmap(lambda row_key: jax.random.permutation(row_key, GX))(row_keys).astype(jnp.int32)
    inverse = jnp.argsort(perms, axis=1, stable=True).astype(jnp.int32)
    cell = (jnp.arange(GY, dtype=jnp.int32)[:, None] * GX + inverse).astype(jnp.int32)
    column = perms.reshape(-1)
    row_of = jnp.repeat(jnp.arange(GY, dtype=jnp.int32), GX)
    east_index = cell[row_of, (column + 1) % GX]
    west_index = cell[row_of, (column + GX - 1) % GX]
    north_index = cell[(row_of + 1) % GY, column]
    south_index = cell[(row_of + GY - 1) % GY, column]
    tables = jnp.stack([east_index, west_index, north_index, south_index]).astype(jnp.int32)
    row_level = jax.random.randint(key_level, (GY,), 0, 4)
    col_level = jax.random.randint(key_cols, (GX,), 0, 4)
    noise = jax.random.randint(key_noise, (POINTS,), 0, 3)
    score = (row_level[row_of] + col_level[column]) * 4 + noise
    order = jnp.argsort(score, stable=True).astype(jnp.int32)
    sea_int = jnp.zeros((POINTS,), jnp.int32).at[order[:WET]].set(1)
    pick = jax.random.randint(key_pick, (POINTS,), 0, 1 << 20)
    pick = jnp.where(sea_int == 1, pick, 1 << 21)
    chosen = jnp.argsort(pick, stable=True).astype(jnp.int32)
    return (tables, sea_int, chosen[:NB], chosen[NB:2 * NB])


def draw_neighbours(key, part):
    return jnp.stack([geometry(key, nest_id)[0] for nest_id in range(NESTS)]).astype(jnp.int32)


def draw_wet_mask(key, part):
    return jnp.stack([geometry(key, nest_id)[1] for nest_id in range(NESTS)]).astype(jnp.int32)


def draw_send_list(key, part):
    return jnp.stack([geometry(key, nest_id)[2] for nest_id in range(NESTS)]).astype(jnp.int32)


def draw_recv_list(key, part):
    return jnp.stack([geometry(key, nest_id)[3] for nest_id in range(NESTS)]).astype(jnp.int32)


def draw_substep_count(key, part):
    base_key = jax.random.fold_in(key, 4421)
    key_big, key_rest = jax.random.split(base_key)
    busiest = jax.random.randint(key_big, (), 0, NESTS)
    others = jax.random.randint(key_rest, (NESTS,), 1, SUBSTEPS + 1)
    return jnp.where(jnp.arange(NESTS) == busiest, SUBSTEPS, others).astype(jnp.int32)


def level_of(rng, extent, pieces, smallest, largest):
    level, own = 1.0, jax.random.fold_in(rng, 6)
    for axis_at, blocks in pieces:
        heights = jnp.exp(jax.random.uniform(jax.random.fold_in(own, axis_at), (blocks,), jnp.float32, smallest / len(pieces), largest / len(pieces)))
        level = level * jnp.repeat(heights, extent[axis_at] // blocks).reshape([-1 if axis == axis_at else 1 for axis in range(len(extent))])
    return level


def centred(stream_key, dims, width, limit, kind=jnp.bfloat16):
    array = width * jax.random.normal(stream_key, dims, jnp.float32)
    return jnp.clip(array, min=-limit, max=limit).astype(kind)


def setup_inputs(seed: int = 0) -> dict:
    seeds = jax.random.split(jax.random.key(seed), 12)
    spectra = jnp.clip(jnp.exp(math.log(2.0) - 3.6888794 * jax.random.uniform(seeds[0], (NESTS, K, POINTS), jnp.float32) ** level_of(seeds[0], (NESTS, K, POINTS), ((0, 2), (1, 128)), -0.2, 0.2)), 0.05, 2.0)
    courant = jnp.clip(jax.random.uniform(seeds[1], (2, K), jnp.float32, -0.9, 0.9) * level_of(seeds[1], (2, K), ((1, 128),), -0.4, 0.0), -0.9, 0.9)
    coupling = centred(seeds[2], (K, K), K ** -0.5, 0.1875)
    growth = jnp.clip(jnp.exp(jax.random.uniform(seeds[3], (K,), jnp.float32, math.log(0.05), math.log(0.5))), 0.05, 0.5)
    dissipation = jnp.clip(jnp.exp(jax.random.uniform(seeds[4], (K,), jnp.float32, math.log(0.2), math.log(2.0))), 0.2, 2.0)
    wind = jnp.clip(0.5 + 1.5 * jax.random.uniform(seeds[5], (NESTS, POINTS), jnp.float32) ** level_of(seeds[5], (NESTS, POINTS), ((0, 2),), -0.2, 0.2), 0.5, 2.0)
    neighbours = draw_neighbours(jax.random.fold_in(seeds[11], 71), 0)
    wet_mask = draw_wet_mask(jax.random.fold_in(seeds[11], 71), 0)
    send_list = draw_send_list(jax.random.fold_in(seeds[11], 71), 0)
    recv_list = draw_recv_list(jax.random.fold_in(seeds[11], 71), 0)
    substep_count = draw_substep_count(jax.random.fold_in(seeds[11], 71), 0)
    return {"spectra": spectra, "courant": courant, "coupling": coupling, "growth": growth, "dissipation": dissipation, "wind": wind, "neighbours": neighbours, "wet_mask": wet_mask, "send_list": send_list, "recv_list": recv_list, "substep_count": substep_count}


source_dt = 0.25
tiny_add = 1e-06

def advect(field, rate, fwd_index, back_index, fwd_next):
    magnitude = jnp.abs(rate)
    forward = rate >= 0.0
    next_cell = field[:, fwd_index]
    prev_cell = field[:, back_index]
    next_next = field[:, fwd_next]
    upwind = jnp.where(forward, field, next_cell)
    downwind = jnp.where(forward, next_cell, field)
    far_upwind = jnp.where(forward, prev_cell, next_next)
    estimate = 0.5 * (upwind + downwind) - 0.5 * magnitude * (downwind - upwind) - (1.0 - magnitude * magnitude) / 6.0 * (downwind - 2.0 * upwind + far_upwind)
    face_value = jnp.clip(estimate, jnp.minimum(upwind, downwind), jnp.maximum(upwind, downwind))
    return field - rate * (face_value - face_value[:, back_index])

def integrate(columns, wind_cols, coupling, growth, dissipation):
    for repeat in range(SRC):
        linear = jnp.dot(coupling, columns.astype(jnp.bfloat16), preferred_element_type=jnp.float32)
        spread = jnp.sqrt(lax.optimization_barrier(jnp.mean(columns * columns, axis=0)) + tiny_add)
        columns = (columns + source_dt * (linear + growth[:, None] * wind_cols[None, :] * columns)) / (1.0 + source_dt * dissipation[:, None] * spread[None, :])
    return columns

def wet_points(sea_int, total):
    position = (jnp.cumsum(sea_int) - 1).astype(jnp.int32)
    target = jnp.where(sea_int == 1, position, total).astype(jnp.int32)
    return jnp.zeros((total,), jnp.int32).at[target].set(jnp.arange(sea_int.shape[0], dtype=jnp.int32), mode='drop')

def reference(spectra, courant, coupling, growth, dissipation, wind, neighbours, wet_mask, send_list, recv_list, substep_count):
    nests = spectra.shape[0]
    bins = spectra.shape[1]
    points = spectra.shape[2]
    sea = wet_mask.astype(jnp.float32)
    east_index = neighbours[:, 0]
    west_index = neighbours[:, 1]
    north_index = neighbours[:, 2]
    south_index = neighbours[:, 3]
    east_next = jnp.take_along_axis(east_index, east_index, axis=1)
    north_next = jnp.take_along_axis(north_index, north_index, axis=1)
    steps_float = substep_count.astype(jnp.float32)

    def propagate(block):
        field, cour = block
        field = field * sea[:, None, :]
        for substep in range(SUBSTEPS):
            incoming = [field[(nest_id + 1) % nests][:, send_list[(nest_id + 1) % nests]] for nest_id in range(nests)]
            updated = []
            for nest_id in range(nests):
                current = field[nest_id].at[:, recv_list[nest_id]].set(incoming[nest_id])
                rates = cour / steps_float[nest_id]
                current = advect(current, rates[0][:, None], east_index[nest_id], west_index[nest_id], east_next[nest_id])
                current = advect(current, rates[1][:, None], north_index[nest_id], south_index[nest_id], north_next[nest_id])
                current = current * sea[nest_id][None, :]
                updated.append(jnp.where(substep < substep_count[nest_id], current, field[nest_id]))
            field = jnp.stack(updated)
        return field
    blocks = spectra.reshape(nests, bins // 8, 8, points).transpose(1, 0, 2, 3)
    cour_blocks = courant.reshape(2, bins // 8, 8).transpose(1, 0, 2)
    moved = lax.map(propagate, (blocks, cour_blocks))
    moved = moved.transpose(1, 0, 2, 3).reshape(nests, bins, points)
    results = []
    for nest_id in range(nests):
        wet_index = wet_points(wet_mask[nest_id], points // 2)
        columns = moved[nest_id][:, wet_index]
        columns = integrate(columns, wind[nest_id][wet_index], coupling, growth, dissipation)
        results.append(jnp.zeros((bins, points), jnp.float32).at[:, wet_index].set(columns))
    return jnp.stack(results)
```

```python
import jax
import jax.numpy as jnp
from jax import lax
from jax.experimental import pallas as pl
from jax.experimental.pallas import tpu as pltpu
from jax.sharding import PartitionSpec as P

SUBSTEPS = 2
SRC = 5
SOURCE_DT = 0.25
TINY = 1e-06
GX = 256
GY = 32
BINS = 9
K = 1152
ROWS = 64
NB = 2048
SLOTS = 32
SOURCES = 128
STAGES = 13
f32, bf16, i32 = jnp.float32, jnp.bfloat16, jnp.int32


def iota(shape, dim):
    return lax.broadcasted_iota(i32, shape, dim)


def lanes(x, index):
    return jnp.take_along_axis(x, index, axis=1, mode="promise_in_bounds")


def pick(table, index):
    low = jnp.concatenate([table[:GY], table[:GY]], 0)
    high = jnp.concatenate([table[GY:], table[GY:]], 0)
    within = index & 127
    return jnp.where(index < 128, lanes(low, within), lanes(high, within))


def load_split(ref, *lead):
    return jnp.concatenate(
        [ref[(*lead, pl.ds(half, GY, stride=2), slice(None))] for half in range(2)], 0
    )


def linear_shift(x, amount):
    if amount >= 128:
        return pltpu.roll(x, ROWS - amount // 128, 0)
    turned = pltpu.roll(x, 128 - amount, 1)
    return jnp.where(iota(x.shape, 1) >= 128 - amount, pltpu.roll(turned, ROWS - 1, 0), turned)


def linear_unshift(x, amount):
    if amount >= 128:
        return pltpu.roll(x, amount // 128, 0)
    turned = pltpu.roll(x, amount, 1)
    return jnp.where(iota(x.shape, 1) < amount, pltpu.roll(turned, 1, 0), turned)


def col_shift(x, amount):
    lane = iota((GY, 128), 1)
    low = pltpu.roll(x[:GY], (128 - amount) % 128, 1)
    high = pltpu.roll(x[GY:], (128 - amount) % 128, 1)
    crossed = lane >= 128 - amount if amount > 0 else lane < -amount
    return jnp.concatenate([jnp.where(crossed, high, low), jnp.where(crossed, low, high)], 0)


def row_shift(x, amount):
    turn = (GY - amount) % GY
    return jnp.concatenate([pltpu.roll(x[:GY], turn, 0), pltpu.roll(x[GY:], turn, 0)], 0)


def advect(field, rate, shift):
    magnitude = jnp.abs(rate)
    forward = rate >= 0.0
    ahead = shift(field, 1)
    upwind = jnp.where(forward, field, ahead)
    downwind = jnp.where(forward, ahead, field)
    far_upwind = jnp.where(forward, shift(field, -1), shift(field, 2))
    estimate = (
        0.5 * (upwind + downwind)
        - 0.5 * magnitude * (downwind - upwind)
        - ((1.0 - magnitude * magnitude) * (1.0 / 6.0)) * (downwind - 2.0 * upwind + far_upwind)
    )
    low, high = jnp.minimum(upwind, downwind), jnp.maximum(upwind, downwind)
    face = jnp.minimum(jnp.maximum(estimate, low), high)
    return field - rate * (face - shift(face, -1))


def two_parts(x):
    high = x.astype(bf16)
    return high, (x - high.astype(f32)).astype(bf16)


def stage_rows(b, x, lhs):
    row = jnp.concatenate([x[:GY], x[GY:]], 1)
    high, rest = two_parts(row)
    lhs[b * GY : (b + 1) * GY, :] = high
    lhs[(BINS + b) * GY : (BINS + b + 1) * GY, :] = rest


def gather_send(send, lhs, out):
    def chunk(c, carry):
        at = pl.ds(pl.multiple_of(c * 256, 256), 256)
        point = send[:, at]
        onehot = (iota((GX, 256), 0) == (point & (GX - 1))).astype(f32).astype(bf16)
        found = jnp.dot(lhs[...], onehot, preferred_element_type=f32)
        mine = iota((GY, 256), 0) == (point // GX)
        rows = []
        for b in range(BINS):
            whole = found[b * GY : (b + 1) * GY] + found[(BINS + b) * GY : (BINS + b + 1) * GY]
            rows.append(jnp.sum(jnp.where(mine, whole, 0.0), axis=0, keepdims=True))
        out[:, at] = jnp.concatenate(rows, 0)
        return carry

    lax.fori_loop(0, NB // 256, chunk, 0, unroll=2)


def start_kernel(
    spectra, tables, wet, wind, send, field, index, sea_out, turn_out, words, wind_out, out, lhs
):
    def table(t, half):
        return tables[pl.ds(t + 4 * half, GY, stride=8), :]

    column = iota((ROWS, 128), 1) + jnp.where(iota((ROWS, 128), 0) >= GY, 128, 0)
    east = jnp.concatenate([table(0, 0), table(0, 1)], 0) & (GX - 1)
    west = jnp.concatenate([table(1, 0), table(1, 1)], 0) & (GX - 1)
    walk = jnp.where(column == 0, 0, west + GX)
    for _ in range(8):
        walk = (walk & -GX) + pick(walk, walk & (GX - 1))
    steps = walk >> 8
    reach, ring = jnp.zeros((ROWS, 128), i32), east
    for k in range(8):
        reach = jnp.where(((column >> k) & 1) == 1, pick(ring, reach), reach)
        if k < 7:
            ring = pick(ring, ring)

    north, south = table(2, 0), table(3, 0)
    upward = jnp.broadcast_to(north[0:1, 0:1], (GY, 128)) // GX == 1
    above = jnp.where(
        upward,
        jnp.broadcast_to(north[:, 0:1], (GY, 128)),
        jnp.broadcast_to(south[:, 0:1], (GY, 128)),
    ) & (GX - 1)
    above = pltpu.roll(above, 1, 0)
    within = above & 127
    offset = jnp.where(above < 128, lanes(steps[:GY], within), lanes(steps[GY:], within))
    offset = jnp.where(iota((GY, 128), 0) == 0, 0, offset)
    ladder = (iota((GY, GY), 1) <= iota((GY, GY), 0)).astype(f32).astype(bf16)
    total = jnp.dot(ladder, offset.astype(f32).astype(bf16), preferred_element_type=f32)
    start = (GX * GY - total.astype(i32)) & (GX - 1)
    start = jnp.concatenate([start, start], 0)
    index[0] = pick(reach, (column - start) & (GX - 1))
    index[1] = (steps + start) & (GX - 1)
    turn_out[...] = jnp.where(upward[:8], 1.0, -1.0)

    wet_int = load_split(wet)
    sea = wet_int.astype(f32)
    sea_out[...] = sea
    for b in range(BINS):
        x = load_split(spectra, b) * sea
        field[b] = x
        stage_rows(b, x, lhs)
    gather_send(send, lhs, out)

    dry = (1.0 - sea).astype(bf16)
    before = (iota((128, 128), 0) < iota((128, 128), 1)).astype(f32).astype(bf16)
    rows = jnp.dot(dry, jnp.ones((128, 128), bf16), preferred_element_type=f32)
    above_rows = (iota((ROWS, ROWS), 1) < iota((ROWS, ROWS), 0)).astype(f32).astype(bf16)
    move = jnp.dot(dry, before, preferred_element_type=f32) + jnp.dot(
        above_rows, rows.astype(bf16), preferred_element_type=f32
    )
    move = jnp.where(wet_int == 1, move.astype(i32), 0)
    windy = load_split(wind)
    leave, enter = jnp.zeros((ROWS, 128), i32), jnp.zeros((ROWS, 128), i32)
    for k in range(STAGES):
        going = (move >> k) & 1
        leave = leave | (going << k)
        other = linear_shift(move, 1 << k)
        coming = (other >> k) & 1
        enter = enter | (coming << k)
        move = jnp.where(coming == 1, other, jnp.where(going == 1, 0, move))
        windy = jnp.where(coming == 1, linear_shift(windy, 1 << k), windy)
    words[0] = leave
    words[1] = enter
    wind_out[...] = windy[:SLOTS]


def receive(incoming, recv, lhs, rhs):
    point = recv[...]
    rhs[...] = (iota((GX, NB), 0) == (point & (GX - 1))).astype(f32).astype(bf16)
    mine = iota((GY, NB), 0) == point // GX
    for b in range(BINS):
        value = incoming[b : b + 1, :]
        high = value.astype(bf16).astype(f32)
        lhs[b * GY : (b + 1) * GY, :] = jnp.where(mine, high, 0.0).astype(bf16)
        lhs[(BINS + b) * GY : (BINS + b + 1) * GY, :] = jnp.where(mine, value - high, 0.0).astype(bf16)
    lhs[2 * BINS * GY :, :] = jnp.where(mine, 1.0, 0.0).astype(bf16)
    return lax.dot_general(
        lhs[...], rhs[...], (((1,), (1,)), ((), ())), preferred_element_type=f32
    )


def substep(number, b, placed, field, courant, count, order, position, sea, turn):
    got = placed[b * GY : (b + 1) * GY] + placed[(BINS + b) * GY : (BINS + b + 1) * GY]
    hit = placed[2 * BINS * GY :]
    got = jnp.concatenate([got[:, :128], got[:, 128:]], 0)
    hit = jnp.concatenate([hit[:, :128], hit[:, 128:]], 0)
    old = field[b]
    x = jnp.where(hit > 0.5, got, old)
    scale = jnp.where(count[0] == 2, 0.5, 1.0)
    x = pick(x, order)
    x = advect(x, jnp.full((ROWS, 128), courant[0, b] * scale), col_shift)
    x = advect(x, (courant[1, b] * scale) * turn, row_shift)
    x = pick(x, position) * sea
    return x if number == 0 else jnp.where(number < count[0], x, old)


def first_kernel(
    incoming, recv, send, field, index, sea, turn, courant, count, field_out, out, lhs, wide, rhs
):
    placed = receive(incoming, recv, wide, rhs)
    turned = jnp.concatenate([turn[...]] * (ROWS // 8), 0)
    for b in range(BINS):
        x = substep(0, b, placed, field, courant, count, index[0], index[1], sea[...], turned)
        field_out[b] = x
        stage_rows(b, x, lhs)
    gather_send(send, lhs, out)


def last_kernel(
    incoming, recv, field, index, sea, turn, words, courant, count, packed, wide, rhs
):
    placed = receive(incoming, recv, wide, rhs)
    turned = jnp.concatenate([turn[...]] * (ROWS // 8), 0)
    enter = words[1]
    for b in range(BINS):
        x = substep(1, b, placed, field, courant, count, index[0], index[1], sea[...], turned)
        for k in range(STAGES):
            x = jnp.where(((enter >> k) & 1) == 1, linear_shift(x, 1 << k), x)
        packed[pl.ds(b, SLOTS, stride=BINS), :] = x[:SLOTS]


def device_of(slot, nest):
    return slot * 4 + lax.rem(2 * nest + 32 - slot // 8 - lax.rem(slot, 8), 4)


def source_kernel(
    packed, coupling, growth, dissipation, wind, back, columns, coarse, grown, damped,
    own_sem, send_sem, recv_sem, back_send, back_recv,
):
    nest, me = lax.axis_index("nest"), lax.axis_index("bin")
    slot = me // 4
    integrates = device_of(slot, nest) == me
    mine = jnp.where(integrates, 1, 0)

    def to(device):
        return {"bin": device}

    def forward(q):
        return pltpu.make_async_remote_copy(
            src_ref=packed.at[pl.ds(q * BINS, BINS)],
            dst_ref=columns.at[pl.ds(me * BINS, BINS)],
            send_sem=send_sem.at[q],
            recv_sem=recv_sem.at[me],
            device_id=to(device_of(q, nest)),
            device_id_type=pl.DeviceIdType.MESH,
        )

    def arriving(s):
        return pltpu.make_async_remote_copy(
            src_ref=packed.at[pl.ds(0, BINS)],
            dst_ref=columns.at[pl.ds(s * BINS, BINS)],
            send_sem=send_sem.at[0],
            recv_sem=recv_sem.at[s],
            device_id=to(s),
            device_id_type=pl.DeviceIdType.MESH,
        )

    def returning(s):
        return pltpu.make_async_remote_copy(
            src_ref=columns.at[pl.ds(s * BINS, BINS)],
            dst_ref=back.at[pl.ds(slot * BINS, BINS)],
            send_sem=back_send.at[s],
            recv_sem=back_recv.at[slot],
            device_id=to(s),
            device_id_type=pl.DeviceIdType.MESH,
        )

    def landing(q):
        return pltpu.make_async_remote_copy(
            src_ref=columns.at[pl.ds(0, BINS)],
            dst_ref=back.at[pl.ds(q * BINS, BINS)],
            send_sem=back_send.at[0],
            recv_sem=back_recv.at[q],
            device_id=to(device_of(q, nest)),
            device_id_type=pl.DeviceIdType.MESH,
        )

    def own_in():
        return pltpu.make_async_copy(
            packed.at[pl.ds(slot * BINS, BINS)], columns.at[pl.ds(me * BINS, BINS)], own_sem
        )

    def own_out():
        return pltpu.make_async_copy(
            columns.at[pl.ds(me * BINS, BINS)], back.at[pl.ds(slot * BINS, BINS)], own_sem
        )

    def each(count, first, skip, body):
        def step(i, carry):
            at = lax.rem(first + i, count)

            @pl.when(at != skip)
            def _():
                body(at)

            return carry

        lax.fori_loop(0, count, step, 0)

    skipped_slot = jnp.where(integrates, slot, -1)
    barrier = pltpu.get_barrier_semaphore()

    @pl.when(integrates)
    def _():
        def greet(s):
            pl.semaphore_signal(
                barrier, inc=1, device_id=to(s), device_id_type=pl.DeviceIdType.MESH
            )

        each(SOURCES, me, me, greet)

    for block in range(BINS):
        at = slice(block * 128, (block + 1) * 128)
        grown[at, :] = jnp.transpose(jnp.broadcast_to(SOURCE_DT * growth[:, at], (128, 128)))
        damped[at, :] = jnp.transpose(jnp.broadcast_to(SOURCE_DT * dissipation[:, at], (128, 128)))

    pl.semaphore_wait(barrier, SLOTS - mine)
    each(SLOTS, slot, skipped_slot, lambda q: forward(q).start())

    @pl.when(integrates)
    def _():
        own_in().start()
        each(SOURCES, me, me, lambda s: arriving(s).wait_recv())
        own_in().wait()
        windy = wind[pl.ds(slot, 1), :]

        def step(i, carry):
            v = columns[...]
            coarse[...] = v.astype(bf16)
            linear = jnp.dot(coupling[...], coarse[...], preferred_element_type=f32)
            rms = jnp.sqrt(jnp.sum(v * v, axis=0, keepdims=True) * (1.0 / K) + TINY)
            columns[...] = (v + (SOURCE_DT * linear + grown[...] * windy * v)) / (
                1.0 + damped[...] * rms
            )
            return carry

        lax.fori_loop(0, SRC, step, 0)
        each(SOURCES, me, me, lambda s: returning(s).start())
        own_out().start()
        own_out().wait()

    each(SLOTS, slot, skipped_slot, lambda q: landing(q).wait_recv())
    each(SLOTS, slot, skipped_slot, lambda q: forward(q).wait_send())

    @pl.when(integrates)
    def _():
        each(SOURCES, me, me, lambda s: returning(s).wait_send())


def finish_kernel(back, words, sea, result):
    leave = words[0]
    wet = sea[...] > 0.5
    for b in range(BINS):
        x = back[pl.ds(b, SLOTS, stride=BINS), :]
        x = jnp.concatenate([x, x], 0)
        for k in reversed(range(STAGES - 1)):
            x = jnp.where(((leave >> k) & 1) == 1, linear_unshift(x, 1 << k), x)
        x = jnp.where(wet, x, 0.0)
        for half in range(2):
            result[b, pl.ds(half, GY, stride=2), :] = x[half * GY : (half + 1) * GY]


def call(kernel, inputs, outputs, scratch=(), scalars=(), **params):
    vmem = pl.BlockSpec(memory_space=pltpu.VMEM)
    smem = pl.BlockSpec(memory_space=pltpu.SMEM)
    return pl.pallas_call(
        kernel,
        out_shape=[jax.ShapeDtypeStruct(*out) for out in outputs],
        in_specs=[vmem] * len(inputs) + [smem] * len(scalars),
        out_specs=[vmem] * len(outputs),
        scratch_shapes=list(scratch),
        compiler_params=pltpu.CompilerParams(**params),
    )(*inputs, *scalars)


def local(
    spectra, courant, coupling, growth, dissipation, wind,
    neighbours, wet_mask, send_list, recv_list, substep_count,
):
    def swap(array):
        return lax.ppermute(array, "nest", [(0, 1), (1, 0)])

    grid = ((BINS, ROWS, 128), f32)
    plane = (ROWS, 128)
    listed = ((BINS, NB), f32)
    lhs = pltpu.VMEM((2 * BINS * GY, GX), bf16)
    wide = pltpu.VMEM((2 * BINS * GY + GY, NB), bf16)
    rhs = pltpu.VMEM((GX, NB), bf16)
    tables = neighbours.reshape(4, ROWS, 128).transpose(1, 0, 2).reshape(4 * ROWS, 128)
    field, index, sea, turn, words, windy, out = call(
        start_kernel,
        [spectra.reshape(BINS, ROWS, 128), tables, wet_mask.reshape(plane), wind.reshape(plane), send_list],
        [grid, ((2, *plane), i32), (plane, f32), ((8, 128), f32), ((2, *plane), i32), ((SLOTS, 128), f32), listed],
        [lhs],
    )
    field, out = call(
        first_kernel,
        [swap(out), recv_list, send_list, field, index, sea, turn],
        [grid, listed],
        [lhs, wide, rhs],
        [courant, substep_count],
    )
    (packed,) = call(
        last_kernel,
        [swap(out), recv_list, field, index, sea, turn, words],
        [((SLOTS * BINS, 128), f32)],
        [wide, rhs],
        [courant, substep_count],
    )
    (back,) = call(
        source_kernel,
        [packed, coupling, growth.reshape(1, K), dissipation.reshape(1, K), windy],
        [((SLOTS * BINS, 128), f32)],
        [
            pltpu.VMEM((K, 128), f32), pltpu.VMEM((K, 128), bf16),
            pltpu.VMEM((K, 128), f32), pltpu.VMEM((K, 128), f32),
            pltpu.SemaphoreType.DMA,
            pltpu.SemaphoreType.DMA((SLOTS,)), pltpu.SemaphoreType.DMA((SOURCES,)),
            pltpu.SemaphoreType.DMA((SOURCES,)), pltpu.SemaphoreType.DMA((SLOTS,)),
        ],
        collective_id=0,
        has_side_effects=True,
    )
    (result,) = call(finish_kernel, [back, words, sea], [grid])
    return result.reshape(1, BINS, ROWS * 128)


def solution(mesh):
    in_specs = (
        P("nest", "bin", None), P(None, "bin"), P(), P(), P(), P("nest", None),
        P("nest", None, None), P("nest", None), P("nest", None), P("nest", None), P("nest"),
    )
    return jax.shard_map(
        local, mesh=mesh, in_specs=in_specs, out_specs=P("nest", "bin", None), check_vma=False
    )
```

```python
import jax
import jax.numpy as jnp
from jax import lax
from jax.experimental import pallas as pl
from jax.experimental.pallas import tpu as pltpu
from jax.sharding import PartitionSpec as P

SUBSTEPS = 2
SRC = 5
SOURCE_DT = 0.25
TINY = 1e-06
GX = 256
GY = 32
BINS = 9
K = 1152
ROWS = 64
NB = 2048
SLOTS = 32
SOURCES = 128
STAGES = 13
f32, bf16, i32 = jnp.float32, jnp.bfloat16, jnp.int32


def iota(shape, dim):
    return lax.broadcasted_iota(i32, shape, dim)


def lanes(x, index):
    return jnp.take_along_axis(x, index, axis=1, mode="promise_in_bounds")


def pick(table, index):
    low = jnp.concatenate([table[:GY], table[:GY]], 0)
    high = jnp.concatenate([table[GY:], table[GY:]], 0)
    within = index & 127
    return jnp.where(index < 128, lanes(low, within), lanes(high, within))


def load_split(ref, *lead):
    return jnp.concatenate(
        [ref[(*lead, pl.ds(half, GY, stride=2), slice(None))] for half in range(2)], 0
    )


def linear_shift(x, amount):
    if amount >= 128:
        return pltpu.roll(x, ROWS - amount // 128, 0)
    turned = pltpu.roll(x, 128 - amount, 1)
    return jnp.where(iota(x.shape, 1) >= 128 - amount, pltpu.roll(turned, ROWS - 1, 0), turned)


def linear_unshift(x, amount):
    if amount >= 128:
        return pltpu.roll(x, amount // 128, 0)
    turned = pltpu.roll(x, amount, 1)
    return jnp.where(iota(x.shape, 1) < amount, pltpu.roll(turned, 1, 0), turned)


def col_shift(x, amount):
    lane = iota((GY, 128), 1)
    low = pltpu.roll(x[:GY], (128 - amount) % 128, 1)
    high = pltpu.roll(x[GY:], (128 - amount) % 128, 1)
    crossed = lane >= 128 - amount if amount > 0 else lane < -amount
    return jnp.concatenate([jnp.where(crossed, high, low), jnp.where(crossed, low, high)], 0)


def row_shift(x, amount):
    turn = (GY - amount) % GY
    return jnp.concatenate([pltpu.roll(x[:GY], turn, 0), pltpu.roll(x[GY:], turn, 0)], 0)


def advect(field, rate, shift):
    magnitude = jnp.abs(rate)
    forward = rate >= 0.0
    ahead = shift(field, 1)
    upwind = jnp.where(forward, field, ahead)
    downwind = jnp.where(forward, ahead, field)
    far_upwind = jnp.where(forward, shift(field, -1), shift(field, 2))
    estimate = (
        0.5 * (upwind + downwind)
        - 0.5 * magnitude * (downwind - upwind)
        - ((1.0 - magnitude * magnitude) * (1.0 / 6.0)) * (downwind - 2.0 * upwind + far_upwind)
    )
    low, high = jnp.minimum(upwind, downwind), jnp.maximum(upwind, downwind)
    face = jnp.minimum(jnp.maximum(estimate, low), high)
    return field - rate * (face - shift(face, -1))


def two_parts(x):
    high = x.astype(bf16)
    return high, (x - high.astype(f32)).astype(bf16)


def stage_rows(b, x, lhs):
    row = jnp.concatenate([x[:GY], x[GY:]], 1)
    high, rest = two_parts(row)
    lhs[b * GY : (b + 1) * GY, :] = high
    lhs[(BINS + b) * GY : (BINS + b + 1) * GY, :] = rest


def gather_send(send, chosen, lhs, out):
    def chunk(c, carry):
        at = pl.ds(pl.multiple_of(c * 256, 256), 256)
        point = send[:, at]
        found = jnp.dot(lhs[...], chosen[:, at], preferred_element_type=f32)
        mine = iota((GY, 256), 0) == (point // GX)
        rows = []
        for b in range(BINS):
            whole = found[b * GY : (b + 1) * GY] + found[(BINS + b) * GY : (BINS + b + 1) * GY]
            rows.append(jnp.sum(jnp.where(mine, whole, 0.0), axis=0, keepdims=True))
        out[:, at] = jnp.concatenate(rows, 0)
        return carry

    lax.fori_loop(0, NB // 256, chunk, 0, unroll=2)


def grid_order(tables):
    def table(t, half):
        return tables[pl.ds(t + 4 * half, GY, stride=8), :]

    column = iota((ROWS, 128), 1) + jnp.where(iota((ROWS, 128), 0) >= GY, 128, 0)
    east = jnp.concatenate([table(0, 0), table(0, 1)], 0) & (GX - 1)
    west = jnp.concatenate([table(1, 0), table(1, 1)], 0) & (GX - 1)
    walk = jnp.where(column == 0, 0, west + GX)
    for _ in range(8):
        walk = (walk & -GX) + pick(walk, walk & (GX - 1))
    steps = walk >> 8
    reach, ring = jnp.zeros((ROWS, 128), i32), east
    for k in range(8):
        reach = jnp.where(((column >> k) & 1) == 1, pick(ring, reach), reach)
        if k < 7:
            ring = pick(ring, ring)

    north, south = table(2, 0), table(3, 0)
    upward = jnp.broadcast_to(north[0:1, 0:1], (GY, 128)) // GX == 1
    above = jnp.where(
        upward,
        jnp.broadcast_to(north[:, 0:1], (GY, 128)),
        jnp.broadcast_to(south[:, 0:1], (GY, 128)),
    ) & (GX - 1)
    above = pltpu.roll(above, 1, 0)
    within = above & 127
    offset = jnp.where(above < 128, lanes(steps[:GY], within), lanes(steps[GY:], within))
    offset = jnp.where(iota((GY, 128), 0) == 0, 0, offset)
    ladder = (iota((GY, GY), 1) <= iota((GY, GY), 0)).astype(f32).astype(bf16)
    total = jnp.dot(ladder, offset.astype(f32).astype(bf16), preferred_element_type=f32)
    start = (GX * GY - total.astype(i32)) & (GX - 1)
    start = jnp.concatenate([start, start], 0)
    order = pick(reach, (column - start) & (GX - 1))
    return order, (steps + start) & (GX - 1), jnp.where(upward[:8], 1.0, -1.0)


def packing(wet_int, windy):
    dry = (1.0 - wet_int.astype(f32)).astype(bf16)
    before = (iota((128, 128), 0) < iota((128, 128), 1)).astype(f32).astype(bf16)
    rows = jnp.dot(dry, jnp.ones((128, 128), bf16), preferred_element_type=f32)
    above_rows = (iota((ROWS, ROWS), 1) < iota((ROWS, ROWS), 0)).astype(f32).astype(bf16)
    move = jnp.dot(dry, before, preferred_element_type=f32) + jnp.dot(
        above_rows, rows.astype(bf16), preferred_element_type=f32
    )
    move = jnp.where(wet_int == 1, move.astype(i32), 0)
    leave, enter = jnp.zeros((ROWS, 128), i32), jnp.zeros((ROWS, 128), i32)
    for k in range(STAGES):
        going = (move >> k) & 1
        leave = leave | (going << k)
        other = linear_shift(move, 1 << k)
        coming = (other >> k) & 1
        enter = enter | (coming << k)
        move = jnp.where(coming == 1, other, jnp.where(going == 1, 0, move))
        windy = jnp.where(coming == 1, linear_shift(windy, 1 << k), windy)
    return leave, enter, windy[:SLOTS]


def receive(incoming, recv, lhs, rhs):
    mine = iota((GY, NB), 0) == recv[...] // GX
    for b in range(BINS):
        value = incoming[b : b + 1, :]
        high = value.astype(bf16).astype(f32)
        lhs[b * GY : (b + 1) * GY, :] = jnp.where(mine, high, 0.0).astype(bf16)
        lhs[(BINS + b) * GY : (BINS + b + 1) * GY, :] = jnp.where(mine, value - high, 0.0).astype(bf16)
    lhs[2 * BINS * GY :, :] = jnp.where(mine, 1.0, 0.0).astype(bf16)
    return lax.dot_general(
        lhs[...], rhs[...], (((1,), (1,)), ((), ())), preferred_element_type=f32
    )


def substep(number, b, placed, field, courant, count, order, position, sea, turn):
    got = placed[b * GY : (b + 1) * GY] + placed[(BINS + b) * GY : (BINS + b + 1) * GY]
    hit = placed[2 * BINS * GY :]
    got = jnp.concatenate([got[:, :128], got[:, 128:]], 0)
    hit = jnp.concatenate([hit[:, :128], hit[:, 128:]], 0)
    old = field[b]
    x = jnp.where(hit > 0.5, got, old)
    scale = jnp.where(count[0] == 2, 0.5, 1.0)
    x = pick(x, order)
    x = advect(x, jnp.full((ROWS, 128), courant[0, b] * scale), col_shift)
    x = advect(x, (courant[1, b] * scale) * turn, row_shift)
    x = pick(x, position) * sea
    return x if number == 0 else jnp.where(number < count[0], x, old)


def device_of(slot, nest):
    return slot * 4 + lax.rem(2 * nest + 32 - slot // 8 - lax.rem(slot, 8), 4)


def step_kernel(
    spectra, tables, wet, wind, send, recv, growth, dissipation, coupling, courant, count, result,
    field, lhs, wide, chosen, placed_at, going, coming, packed, windy,
    columns, coarse, grown, damped, weights, back,
    weight_sem, swap_send, swap_recv, own_sem, send_sem, recv_sem, back_send, back_recv,
):
    nest, me = lax.axis_index("nest"), lax.axis_index("bin")
    slot = me // 4
    integrates = device_of(slot, nest) == me
    mine = jnp.where(integrates, 1, 0)

    def to(device):
        return {"bin": device}

    def forward(q):
        return pltpu.make_async_remote_copy(
            src_ref=packed.at[pl.ds(q * BINS, BINS)],
            dst_ref=columns.at[pl.ds(me * BINS, BINS)],
            send_sem=send_sem,
            recv_sem=recv_sem,
            device_id=to(device_of(q, nest)),
            device_id_type=pl.DeviceIdType.MESH,
        )

    def returning(s):
        return pltpu.make_async_remote_copy(
            src_ref=columns.at[pl.ds(s * BINS, BINS)],
            dst_ref=back.at[pl.ds(slot * BINS, BINS)],
            send_sem=back_send,
            recv_sem=back_recv,
            device_id=to(s),
            device_id_type=pl.DeviceIdType.MESH,
        )

    def several(count, ref, sent, received):
        rows = ref.at[pl.ds(0, count * BINS)]
        return pltpu.make_async_remote_copy(
            src_ref=rows,
            dst_ref=rows,
            send_sem=sent,
            recv_sem=received,
            device_id=to(lax.rem(me + 1, SOURCES)),
            device_id_type=pl.DeviceIdType.MESH,
        )

    def own_in():
        return pltpu.make_async_copy(
            packed.at[pl.ds(slot * BINS, BINS)], columns.at[pl.ds(me * BINS, BINS)], own_sem
        )

    def own_out():
        return pltpu.make_async_copy(
            columns.at[pl.ds(me * BINS, BINS)], back.at[pl.ds(slot * BINS, BINS)], own_sem
        )

    def others(count, own):
        return [lax.rem(own + i, count) for i in range(1, count)]

    def swap(number):
        return pltpu.make_async_remote_copy(
            src_ref=going.at[number],
            dst_ref=coming.at[number],
            send_sem=swap_send.at[number],
            recv_sem=swap_recv.at[number],
            device_id={"nest": 1 - nest},
            device_id_type=pl.DeviceIdType.MESH,
        )

    barrier = pltpu.get_barrier_semaphore()
    pl.semaphore_signal(
        barrier, inc=1, device_id={"nest": 1 - nest}, device_id_type=pl.DeviceIdType.MESH
    )

    @pl.when(integrates)
    def _():
        for s in others(SOURCES, me):
            pl.semaphore_signal(
                barrier, inc=1, device_id=to(s), device_id_type=pl.DeviceIdType.MESH
            )

    fetch = pltpu.make_async_copy(coupling, weights, weight_sem)
    fetch.start()

    wet_int = load_split(wet)
    sea = wet_int.astype(f32)
    for b in range(BINS):
        x = load_split(spectra, b) * sea
        field[b] = x
        stage_rows(b, x, lhs)
    chosen[...] = (iota((GX, NB), 0) == (send[...] & (GX - 1))).astype(f32).astype(bf16)
    placed_at[...] = (iota((GX, NB), 0) == (recv[...] & (GX - 1))).astype(f32).astype(bf16)
    gather_send(send, chosen, lhs, going.at[0])
    order, position, turn = grid_order(tables)
    turn = jnp.concatenate([turn] * (ROWS // 8), 0)

    pl.semaphore_wait(barrier, SLOTS - mine + 1)
    swap(0).start()
    leave, enter, windy[...] = packing(wet_int, load_split(wind))
    swap(0).wait_recv()

    placed = receive(coming.at[0], recv, wide, placed_at)
    for b in range(BINS):
        x = substep(0, b, placed, field, courant, count, order, position, sea, turn)
        field[b] = x
        stage_rows(b, x, lhs)
    gather_send(send, chosen, lhs, going.at[1])
    swap(1).start()
    for block in range(BINS):
        at = slice(block * 128, (block + 1) * 128)
        grown[at, :] = jnp.transpose(jnp.broadcast_to((SOURCE_DT * growth[at]).reshape(1, 128), (128, 128)))
        damped[at, :] = jnp.transpose(jnp.broadcast_to((SOURCE_DT * dissipation[at]).reshape(1, 128), (128, 128)))
    swap(1).wait_recv()

    placed = receive(coming.at[1], recv, wide, placed_at)
    for b in range(BINS):
        x = substep(1, b, placed, field, courant, count, order, position, sea, turn)
        for k in range(STAGES):
            x = jnp.where(((enter >> k) & 1) == 1, linear_shift(x, 1 << k), x)
        packed[pl.ds(b, SLOTS, stride=BINS), :] = x[:SLOTS]

    for q in others(SLOTS, slot):
        forward(q).start()
    fetch.wait()

    @pl.when(jnp.logical_not(integrates))
    def _():
        forward(slot).start()

    @pl.when(integrates)
    def _():
        own_in().start()
        several(SOURCES - 1, columns, send_sem, recv_sem).wait_recv()
        own_in().wait()
        blown = windy[pl.ds(slot, 1), :]

        def step(i, carry):
            v = columns[...]
            coarse[...] = v.astype(bf16)
            linear = jnp.dot(weights[...], coarse[...], preferred_element_type=f32)
            rms = jnp.sqrt(jnp.sum(v * v, axis=0, keepdims=True) * (1.0 / K) + TINY)
            columns[...] = (v + (SOURCE_DT * linear + grown[...] * blown * v)) / (
                1.0 + damped[...] * rms
            )
            return carry

        lax.fori_loop(0, SRC, step, 0)
        for s in others(SOURCES, me):
            returning(s).start()
        own_out().start()
        own_out().wait()
        several(SLOTS - 1, back, back_send, back_recv).wait_recv()

    @pl.when(jnp.logical_not(integrates))
    def _():
        several(SLOTS, back, back_send, back_recv).wait_recv()

    wet_here = sea > 0.5
    for b in range(BINS):
        x = back[pl.ds(b, SLOTS, stride=BINS), :]
        x = jnp.concatenate([x, x], 0)
        for k in reversed(range(STAGES - 1)):
            x = jnp.where(((leave >> k) & 1) == 1, linear_unshift(x, 1 << k), x)
        x = jnp.where(wet_here, x, 0.0)
        for half in range(2):
            result[b, pl.ds(half, GY, stride=2), :] = x[half * GY : (half + 1) * GY]

    for number in range(SUBSTEPS):
        swap(number).wait_send()

    @pl.when(integrates)
    def _():
        several(SLOTS - 1, packed, send_sem, recv_sem).wait_send()
        several(SOURCES - 1, columns, back_send, back_recv).wait_send()

    @pl.when(jnp.logical_not(integrates))
    def _():
        several(SLOTS, packed, send_sem, recv_sem).wait_send()


def local(
    spectra, courant, coupling, growth, dissipation, wind,
    neighbours, wet_mask, send_list, recv_list, substep_count,
):
    plane = (ROWS, 128)
    tables = neighbours.reshape(4, ROWS, 128).transpose(1, 0, 2).reshape(4 * ROWS, 128)
    vmem = pl.BlockSpec(memory_space=pltpu.VMEM)
    smem = pl.BlockSpec(memory_space=pltpu.SMEM)
    result = pl.pallas_call(
        step_kernel,
        out_shape=jax.ShapeDtypeStruct((BINS, ROWS, 128), f32),
        in_specs=[vmem] * 8 + [pl.BlockSpec(memory_space=pl.ANY), smem, smem],
        out_specs=vmem,
        scratch_shapes=[
            pltpu.VMEM((BINS, ROWS, 128), f32),
            pltpu.VMEM((2 * BINS * GY, GX), bf16),
            pltpu.VMEM((2 * BINS * GY + GY, NB), bf16),
            pltpu.VMEM((GX, NB), bf16),
            pltpu.VMEM((GX, NB), bf16),
            pltpu.VMEM((SUBSTEPS, BINS, NB), f32),
            pltpu.VMEM((SUBSTEPS, BINS, NB), f32),
            pltpu.VMEM((SLOTS * BINS, 128), f32),
            pltpu.VMEM((SLOTS, 128), f32),
            pltpu.VMEM((K, 128), f32),
            pltpu.VMEM((K, 128), bf16),
            pltpu.VMEM((K, 128), f32),
            pltpu.VMEM((K, 128), f32),
            pltpu.VMEM((K, K), bf16),
            pltpu.VMEM((SLOTS * BINS, 128), f32),
            pltpu.SemaphoreType.DMA,
            pltpu.SemaphoreType.DMA((SUBSTEPS,)),
            pltpu.SemaphoreType.DMA((SUBSTEPS,)),
            pltpu.SemaphoreType.DMA,
            pltpu.SemaphoreType.DMA,
            pltpu.SemaphoreType.DMA,
            pltpu.SemaphoreType.DMA,
            pltpu.SemaphoreType.DMA,
        ],
        compiler_params=pltpu.CompilerParams(collective_id=0, has_side_effects=True),
    )(
        spectra.reshape(BINS, ROWS, 128), tables, wet_mask.reshape(plane), wind.reshape(plane),
        send_list, recv_list, growth, dissipation, coupling,
        courant, substep_count,
    )
    return result.reshape(1, BINS, ROWS * 128)


def solution(mesh):
    in_specs = (
        P("nest", "bin", None), P(None, "bin"), P(), P(), P(), P("nest", None),
        P("nest", None, None), P("nest", None), P("nest", None), P("nest", None), P("nest"),
    )
    return jax.shard_map(
        local, mesh=mesh, in_specs=in_specs, out_specs=P("nest", "bin", None), check_vma=False
    )
```

```python
import jax
import jax.numpy as jnp
from jax import lax
from jax.experimental import pallas as pl
from jax.experimental.pallas import tpu as pltpu
from jax.sharding import PartitionSpec as P

SUBSTEPS = 2
SRC = 5
SOURCE_DT = 0.25
TINY = 1e-06
GX = 256
GY = 32
BINS = 9
K = 1152
ROWS = 64
NB = 2048
SLOTS = 32
SOURCES = 128
STAGES = 13
f32, bf16, i32 = jnp.float32, jnp.bfloat16, jnp.int32


def iota(shape, dim):
    return lax.broadcasted_iota(i32, shape, dim)


def lanes(x, index):
    return jnp.take_along_axis(x, index, axis=1, mode="promise_in_bounds")


def pick(table, index):
    low = jnp.concatenate([table[:GY], table[:GY]], 0)
    high = jnp.concatenate([table[GY:], table[GY:]], 0)
    within = index & 127
    return jnp.where(index < 128, lanes(low, within), lanes(high, within))


def load_split(ref, *lead):
    return jnp.concatenate(
        [ref[(*lead, pl.ds(half, GY, stride=2), slice(None))] for half in range(2)], 0
    )


def linear_shift(x, amount):
    if amount >= 128:
        return pltpu.roll(x, ROWS - amount // 128, 0)
    turned = pltpu.roll(x, 128 - amount, 1)
    return jnp.where(iota(x.shape, 1) >= 128 - amount, pltpu.roll(turned, ROWS - 1, 0), turned)


def linear_unshift(x, amount):
    if amount >= 128:
        return pltpu.roll(x, amount // 128, 0)
    turned = pltpu.roll(x, amount, 1)
    return jnp.where(iota(x.shape, 1) < amount, pltpu.roll(turned, 1, 0), turned)


def col_shift(x, amount):
    lane = iota((GY, 128), 1)
    low = pltpu.roll(x[:GY], (128 - amount) % 128, 1)
    high = pltpu.roll(x[GY:], (128 - amount) % 128, 1)
    crossed = lane >= 128 - amount if amount > 0 else lane < -amount
    return jnp.concatenate([jnp.where(crossed, high, low), jnp.where(crossed, low, high)], 0)


def row_shift(x, amount):
    turn = (GY - amount) % GY
    return jnp.concatenate([pltpu.roll(x[:GY], turn, 0), pltpu.roll(x[GY:], turn, 0)], 0)


def advect(field, rate, shift):
    magnitude = jnp.abs(rate)
    forward = rate >= 0.0
    ahead = shift(field, 1)
    upwind = jnp.where(forward, field, ahead)
    downwind = jnp.where(forward, ahead, field)
    far_upwind = jnp.where(forward, shift(field, -1), shift(field, 2))
    estimate = (
        0.5 * (upwind + downwind)
        - 0.5 * magnitude * (downwind - upwind)
        - ((1.0 - magnitude * magnitude) * (1.0 / 6.0)) * (downwind - 2.0 * upwind + far_upwind)
    )
    low, high = jnp.minimum(upwind, downwind), jnp.maximum(upwind, downwind)
    face = jnp.minimum(jnp.maximum(estimate, low), high)
    return field - rate * (face - shift(face, -1))


def onehot(within):
    rows = iota((GX, NB), 0).astype(f32).astype(bf16)
    return jnp.where(rows == within.astype(f32).astype(bf16), jnp.ones((), bf16), jnp.zeros((), bf16))


def two_parts(x):
    high = x.astype(bf16)
    return high, (x - high.astype(f32)).astype(bf16)


def stage_rows(b, x, lhs):
    row = jnp.concatenate([x[:GY], x[GY:]], 1)
    high, rest = two_parts(row)
    lhs[b * GY : (b + 1) * GY, :] = high
    lhs[(BINS + b) * GY : (BINS + b + 1) * GY, :] = rest


def gather_send(send, chosen, lhs, out):
    for c in range(NB // 256):
        at = slice(c * 256, (c + 1) * 256)
        point = send[:, at]
        found = jnp.dot(lhs[...], chosen[:, at], preferred_element_type=f32)
        mine = iota((GY, 256), 0) == (point >> 8)
        rows = []
        for b in range(BINS):
            whole = found[b * GY : (b + 1) * GY] + found[(BINS + b) * GY : (BINS + b + 1) * GY]
            rows.append(jnp.sum(jnp.where(mine, whole, 0.0), axis=0, keepdims=True))
        out[:, at] = jnp.concatenate(rows, 0)


def grid_order(tables):
    def table(t, half):
        return tables[pl.ds(t + 4 * half, GY, stride=8), :]

    column = iota((ROWS, 128), 1) + jnp.where(iota((ROWS, 128), 0) >= GY, 128, 0)
    east = jnp.concatenate([table(0, 0), table(0, 1)], 0) & (GX - 1)
    west = jnp.concatenate([table(1, 0), table(1, 1)], 0) & (GX - 1)
    walk = jnp.where(column == 0, 0, west + GX)
    for _ in range(8):
        walk = (walk & -GX) + pick(walk, walk & (GX - 1))
    steps = walk >> 8
    reach, ring = jnp.zeros((ROWS, 128), i32), east
    for k in range(8):
        reach = jnp.where(((column >> k) & 1) == 1, pick(ring, reach), reach)
        if k < 7:
            ring = pick(ring, ring)

    north, south = table(2, 0), table(3, 0)
    upward = jnp.broadcast_to(north[0:1, 0:1], (GY, 128)) // GX == 1
    above = jnp.where(
        upward,
        jnp.broadcast_to(north[:, 0:1], (GY, 128)),
        jnp.broadcast_to(south[:, 0:1], (GY, 128)),
    ) & (GX - 1)
    above = pltpu.roll(above, 1, 0)
    within = above & 127
    offset = jnp.where(above < 128, lanes(steps[:GY], within), lanes(steps[GY:], within))
    offset = jnp.where(iota((GY, 128), 0) == 0, 0, offset)
    ladder = (iota((GY, GY), 1) <= iota((GY, GY), 0)).astype(f32).astype(bf16)
    total = jnp.dot(ladder, offset.astype(f32).astype(bf16), preferred_element_type=f32)
    start = (GX * GY - total.astype(i32)) & (GX - 1)
    start = jnp.concatenate([start, start], 0)
    order = pick(reach, (column - start) & (GX - 1))
    return order, (steps + start) & (GX - 1), jnp.where(upward[:8], 1.0, -1.0)


def packing(wet_int, windy):
    dry = (1.0 - wet_int.astype(f32)).astype(bf16)
    before = (iota((128, 128), 0) < iota((128, 128), 1)).astype(f32).astype(bf16)
    rows = jnp.dot(dry, jnp.ones((128, 128), bf16), preferred_element_type=f32)
    above_rows = (iota((ROWS, ROWS), 1) < iota((ROWS, ROWS), 0)).astype(f32).astype(bf16)
    move = jnp.dot(dry, before, preferred_element_type=f32) + jnp.dot(
        above_rows, rows.astype(bf16), preferred_element_type=f32
    )
    move = jnp.where(wet_int == 1, move.astype(i32), 0)
    leave, enter = jnp.zeros((ROWS, 128), i32), jnp.zeros((ROWS, 128), i32)
    for k in range(STAGES):
        going = (move >> k) & 1
        leave = leave | (going << k)
        other = linear_shift(move, 1 << k)
        coming = (other >> k) & 1
        enter = enter | (coming << k)
        move = jnp.where(coming == 1, other, jnp.where(going == 1, 0, move))
        windy = jnp.where(coming == 1, linear_shift(windy, 1 << k), windy)
    return leave, enter, windy[:SLOTS]


def receive(incoming, recv, lhs, rhs):
    row = (recv[...] >> 8).astype(f32).astype(bf16)
    mine = iota((GY, NB), 0).astype(f32).astype(bf16) == row
    zero = jnp.zeros((), bf16)
    for b in range(BINS):
        high, rest = two_parts(incoming[b : b + 1, :])
        lhs[b * GY : (b + 1) * GY, :] = jnp.where(mine, jnp.broadcast_to(high, (GY, NB)), zero)
        lhs[(BINS + b) * GY : (BINS + b + 1) * GY, :] = jnp.where(
            mine, jnp.broadcast_to(rest, (GY, NB)), zero
        )
    lhs[2 * BINS * GY :, :] = jnp.where(mine, jnp.ones((), bf16), zero)
    return lax.dot_general(
        lhs[...], rhs[...], (((1,), (1,)), ((), ())), preferred_element_type=f32
    )


def pick_each(tables, index):
    parts = [[] for _ in tables]
    for at in range(0, ROWS, 8):
        low = at % GY
        here = index[at : at + 8]
        within, first = here & 127, here < 128
        for part, table in zip(parts, tables):
            part.append(
                jnp.where(
                    first,
                    lanes(table[low : low + 8], within),
                    lanes(table[GY + low : GY + low + 8], within),
                )
            )
    return [jnp.concatenate(part, 0) for part in parts]


def substep(number, placed, field, courant, count, order, position, sea, turn):
    hit = placed[2 * BINS * GY :]
    hit = jnp.concatenate([hit[:, :128], hit[:, 128:]], 0) > 0.5
    scale = jnp.where(jnp.broadcast_to(count, (ROWS, 128)) == 2, 0.5, 1.0)
    xs = []
    for b in range(BINS):
        got = placed[b * GY : (b + 1) * GY] + placed[(BINS + b) * GY : (BINS + b + 1) * GY]
        xs.append(jnp.where(hit, jnp.concatenate([got[:, :128], got[:, 128:]], 0), field[b]))
    xs = pick_each(xs, order)
    for b in range(BINS):
        x = advect(xs[b], scale * courant[0, b], col_shift)
        xs[b] = advect(x, (scale * turn) * courant[1, b], row_shift)
    xs = [x * sea for x in pick_each(xs, position)]
    if number > 0:
        still = jnp.broadcast_to(count, (ROWS, 128)) > number
        xs = [jnp.where(still, x, field[b]) for b, x in enumerate(xs)]
    return xs


def step_kernel(
    spectra, tables, wet, wind, send, recv, growth, dissipation, substeps, coupling, courant, result,
    field, lhs, wide, chosen, placed_at, going, coming, packed, windy,
    columns, coarse, grown, damped, weights, back,
    weight_sem, swap_send, swap_recv, own_sem, send_sem, recv_sem, back_send, back_recv,
    plane_sem, all_sem,
):
    nest, me = lax.axis_index("nest"), lax.axis_index("bin")
    slot = lax.div(me, 4)
    y, z, x_me = lax.div(me, 32), lax.rem(slot, 8), lax.rem(me, 4)
    ys = [lax.rem(y + d, 4) for d in range(4)]
    zs = [lax.rem(z + d, 8) for d in range(8)]
    xs_at = [lax.rem(x_me + d, 4) for d in range(4)]

    def integrator(dy, dz):
        q = ys[dy] * 8 + zs[dz]
        return q, q * 4 + lax.rem(2 * nest + 32 - ys[dy] - zs[dz], 4)

    def peer(dy, dz, dx):
        return ys[dy] * 32 + zs[dz] * 4 + xs_at[dx]

    far = [0, 1, 2, 3, 4, 3, 2, 1]
    near = [0, 1, 2, 1]
    slots = sorted(
        [(dy, dz) for dy in range(4) for dz in range(8)], key=lambda d: -(near[d[0]] + far[d[1]])
    )[:-1]
    sources = sorted(
        [(dy, dz, dx) for dy in range(4) for dz in range(8) for dx in range(4)],
        key=lambda d: -(near[d[0]] + far[d[1]] + near[d[2]]),
    )[:-1]
    own_device = integrator(0, 0)[1]
    integrates = own_device == me

    def to(device):
        return {"bin": device}

    def forward(q, device):
        return pltpu.make_async_remote_copy(
            src_ref=packed.at[pl.ds(q * BINS, BINS)],
            dst_ref=columns.at[pl.ds(me * BINS, BINS)],
            send_sem=send_sem,
            recv_sem=recv_sem,
            device_id=to(device),
            device_id_type=pl.DeviceIdType.MESH,
        )

    def returning(s):
        return pltpu.make_async_remote_copy(
            src_ref=columns.at[pl.ds(s * BINS, BINS)],
            dst_ref=back.at[pl.ds(slot * BINS, BINS)],
            send_sem=back_send,
            recv_sem=back_recv,
            device_id=to(s),
            device_id_type=pl.DeviceIdType.MESH,
        )

    def several(count, ref, sent, received):
        rows = ref.at[pl.ds(0, count * BINS)]
        return pltpu.make_async_remote_copy(
            src_ref=rows,
            dst_ref=rows,
            send_sem=sent,
            recv_sem=received,
            device_id=to(lax.rem(me + 1, SOURCES)),
            device_id_type=pl.DeviceIdType.MESH,
        )

    def own_in():
        return pltpu.make_async_copy(
            packed.at[pl.ds(slot * BINS, BINS)], columns.at[pl.ds(me * BINS, BINS)], own_sem
        )

    def own_out():
        return pltpu.make_async_copy(
            columns.at[pl.ds(me * BINS, BINS)], back.at[pl.ds(slot * BINS, BINS)], own_sem
        )

    def swap(number):
        return pltpu.make_async_remote_copy(
            src_ref=going.at[number],
            dst_ref=coming.at[number],
            send_sem=swap_send.at[number],
            recv_sem=swap_recv.at[number],
            device_id={"nest": 1 - nest},
            device_id_type=pl.DeviceIdType.MESH,
        )

    def signal(semaphore, device):
        pl.semaphore_signal(
            semaphore, inc=1, device_id=device, device_id_type=pl.DeviceIdType.MESH
        )

    line_x = [to(peer(0, 0, d)) for d in range(1, 4)]
    line_y = [to(peer(d, 0, 0)) for d in range(1, 4)]
    line_z = [to(peer(0, d, 0)) for d in range(1, 8)]
    barrier = pltpu.get_barrier_semaphore()
    for device in line_z + line_y + line_x + [{"nest": 1 - nest}]:
        signal(barrier, device)

    fetch = pltpu.make_async_copy(coupling, weights, weight_sem)
    fetch.start()

    wet_int = load_split(wet)
    sea = wet_int.astype(f32)
    for b in range(BINS):
        x = load_split(spectra, b) * sea
        field[b] = x
        stage_rows(b, x, lhs)
    chosen[...] = onehot(send[...] & (GX - 1))
    placed_at[...] = onehot(recv[...] & (GX - 1))
    gather_send(send, chosen, lhs, going.at[0])
    order, position, turn = grid_order(tables)
    turn = jnp.concatenate([turn] * (ROWS // 8), 0)

    pl.semaphore_wait(barrier, 14)
    swap(0).start()
    for device in line_y:
        signal(plane_sem, device)
    leave, enter, windy[...] = packing(wet_int, load_split(wind))
    swap(0).wait_recv()

    count = substeps[...].reshape(1, 1)
    placed = receive(coming.at[0], recv, wide, placed_at)
    for b, x in enumerate(substep(0, placed, field, courant, count, order, position, sea, turn)):
        field[b] = x
        stage_rows(b, x, lhs)
    gather_send(send, chosen, lhs, going.at[1])
    pl.semaphore_wait(plane_sem, 3)
    for device in line_z:
        signal(all_sem, device)
    swap(1).start()
    for block in range(BINS):
        at = slice(block * 128, (block + 1) * 128)
        grown[at, :] = jnp.transpose(jnp.broadcast_to((SOURCE_DT * growth[at]).reshape(1, 128), (128, 128)))
        damped[at, :] = jnp.transpose(jnp.broadcast_to((SOURCE_DT * dissipation[at]).reshape(1, 128), (128, 128)))
    swap(1).wait_recv()

    placed = receive(coming.at[1], recv, wide, placed_at)
    for b, x in enumerate(substep(1, placed, field, courant, count, order, position, sea, turn)):
        for k in range(STAGES):
            x = jnp.where(((enter >> k) & 1) == 1, linear_shift(x, 1 << k), x)
        packed[pl.ds(b, SLOTS, stride=BINS), :] = x[:SLOTS]

    pl.semaphore_wait(all_sem, 7)
    for offset in slots:
        forward(*integrator(*offset)).start()
    fetch.wait()

    @pl.when(jnp.logical_not(integrates))
    def _():
        forward(slot, own_device).start()

    @pl.when(integrates)
    def _():
        own_in().start()
        several(SOURCES - 1, columns, send_sem, recv_sem).wait_recv()
        own_in().wait()
        blown = windy[pl.ds(slot, 1), :]

        def step(i, carry):
            v = columns[...]
            coarse[...] = v.astype(bf16)
            linear = jnp.dot(weights[...], coarse[...], preferred_element_type=f32)
            rms = jnp.sqrt(jnp.sum(v * v, axis=0, keepdims=True) * (1.0 / K) + TINY)
            columns[...] = (v + (SOURCE_DT * linear + grown[...] * blown * v)) / (
                1.0 + damped[...] * rms
            )
            return carry

        lax.fori_loop(0, SRC, step, 0)
        for offset in sources:
            returning(peer(*offset)).start()
        own_out().start()
        own_out().wait()
        several(SLOTS - 1, back, back_send, back_recv).wait_recv()

    @pl.when(jnp.logical_not(integrates))
    def _():
        several(SLOTS, back, back_send, back_recv).wait_recv()

    for b in range(BINS):
        x = back[pl.ds(b, SLOTS, stride=BINS), :]
        x = jnp.concatenate([x, x], 0)
        for k in reversed(range(STAGES - 1)):
            x = jnp.where(((leave >> k) & 1) == 1, linear_unshift(x, 1 << k), x)
        for half in range(2):
            result[b, pl.ds(half, GY, stride=2), :] = x[half * GY : (half + 1) * GY]

    for number in range(SUBSTEPS):
        swap(number).wait_send()

    @pl.when(integrates)
    def _():
        several(SLOTS - 1, packed, send_sem, recv_sem).wait_send()
        several(SOURCES - 1, columns, back_send, back_recv).wait_send()

    @pl.when(jnp.logical_not(integrates))
    def _():
        several(SLOTS, packed, send_sem, recv_sem).wait_send()


def local(
    spectra, courant, coupling, growth, dissipation, wind,
    neighbours, wet_mask, send_list, recv_list, substep_count,
):
    plane = (ROWS, 128)
    tables = neighbours.reshape(4, ROWS, 128).transpose(1, 0, 2).reshape(4 * ROWS, 128)
    vmem = pl.BlockSpec(memory_space=pltpu.VMEM)
    smem = pl.BlockSpec(memory_space=pltpu.SMEM)
    result = pl.pallas_call(
        step_kernel,
        out_shape=jax.ShapeDtypeStruct((BINS, ROWS, 128), f32),
        in_specs=[vmem] * 9 + [pl.BlockSpec(memory_space=pl.ANY), smem],
        out_specs=vmem,
        scratch_shapes=[
            pltpu.VMEM((BINS, ROWS, 128), f32),
            pltpu.VMEM((2 * BINS * GY, GX), bf16),
            pltpu.VMEM((2 * BINS * GY + GY, NB), bf16),
            pltpu.VMEM((GX, NB), bf16),
            pltpu.VMEM((GX, NB), bf16),
            pltpu.VMEM((SUBSTEPS, BINS, NB), f32),
            pltpu.VMEM((SUBSTEPS, BINS, NB), f32),
            pltpu.VMEM((SLOTS * BINS, 128), f32),
            pltpu.VMEM((SLOTS, 128), f32),
            pltpu.VMEM((K, 128), f32),
            pltpu.VMEM((K, 128), bf16),
            pltpu.VMEM((K, 128), f32),
            pltpu.VMEM((K, 128), f32),
            pltpu.VMEM((K, K), bf16),
            pltpu.VMEM((SLOTS * BINS, 128), f32),
            pltpu.SemaphoreType.DMA,
            pltpu.SemaphoreType.DMA((SUBSTEPS,)),
            pltpu.SemaphoreType.DMA((SUBSTEPS,)),
            pltpu.SemaphoreType.DMA,
            pltpu.SemaphoreType.DMA,
            pltpu.SemaphoreType.DMA,
            pltpu.SemaphoreType.DMA,
            pltpu.SemaphoreType.DMA,
            pltpu.SemaphoreType.REGULAR,
            pltpu.SemaphoreType.REGULAR,
        ],
        compiler_params=pltpu.CompilerParams(collective_id=0, has_side_effects=True),
    )(
        spectra.reshape(BINS, ROWS, 128), tables, wet_mask.reshape(plane), wind.reshape(plane),
        send_list, recv_list, growth, dissipation,
        substep_count, coupling, courant,
    )
    result = jnp.where(wet_mask.reshape(plane)[None] == 1, result, 0.0)
    return result.reshape(1, BINS, ROWS * 128)


def solution(mesh):
    in_specs = (
        P("nest", "bin", None), P(None, "bin"), P(), P(), P(), P("nest", None),
        P("nest", None, None), P("nest", None), P("nest", None), P("nest", None), P("nest"),
    )
    return jax.shard_map(
        local, mesh=mesh, in_specs=in_specs, out_specs=P("nest", "bin", None), check_vma=False
    )
```

```python
import jax
import jax.numpy as jnp
from jax import lax
from jax.experimental import pallas as pl
from jax.experimental.pallas import tpu as pltpu
from jax.sharding import PartitionSpec as P

SUBSTEPS = 2
SRC = 5
SOURCE_DT = 0.25
TINY = 1e-06
GX = 256
GY = 32
BINS = 9
K = 1152
ROWS = 64
NB = 2048
HALF = 1024
SLOTS = 32
SOURCES = 128
STAGES = 13
LANE_STAGES = 7
f32, bf16, i32 = jnp.float32, jnp.bfloat16, jnp.int32


def iota(shape, dim):
    return lax.broadcasted_iota(i32, shape, dim)


def lanes(x, index):
    return jnp.take_along_axis(x, index, axis=1, mode="promise_in_bounds")


def pick(table, index):
    low = jnp.concatenate([table[:GY], table[:GY]], 0)
    high = jnp.concatenate([table[GY:], table[GY:]], 0)
    within = index & 127
    return jnp.where(index < 128, lanes(low, within), lanes(high, within))


def load_split(ref, *lead):
    return jnp.concatenate(
        [ref[(*lead, pl.ds(half, GY, stride=2), slice(None))] for half in range(2)], 0
    )


def linear_shift(x, amount):
    if amount >= 128:
        return pltpu.roll(x, ROWS - amount // 128, 0)
    turned = pltpu.roll(x, 128 - amount, 1)
    return jnp.where(iota(x.shape, 1) >= 128 - amount, pltpu.roll(turned, ROWS - 1, 0), turned)


def rows_unshift(x, amount):
    return pltpu.roll(x, amount // 128, 0)


def choose_each(firsts, seconds, lane, use_first):
    parts = [[] for _ in firsts]
    for at in range(0, ROWS, 8):
        low = at % firsts[0].shape[0]
        within, mask = lane[at : at + 8], use_first[at : at + 8]
        for part, first, second in zip(parts, firsts, seconds):
            part.append(
                jnp.where(mask, lanes(first[low : low + 8], within), lanes(second[low : low + 8], within))
            )
    return [jnp.concatenate(part, 0) for part in parts]


def pick_each(tables, index):
    return choose_each(
        [table[:GY] for table in tables], [table[GY:] for table in tables], index & 127, index < 128
    )


def col_shift(x, amount):
    lane = iota((GY, 128), 1)
    low = pltpu.roll(x[:GY], (128 - amount) % 128, 1)
    high = pltpu.roll(x[GY:], (128 - amount) % 128, 1)
    crossed = lane >= 128 - amount if amount > 0 else lane < -amount
    return jnp.concatenate([jnp.where(crossed, high, low), jnp.where(crossed, low, high)], 0)


def row_shift(x, amount):
    turn = (GY - amount) % GY
    return jnp.concatenate([pltpu.roll(x[:GY], turn, 0), pltpu.roll(x[GY:], turn, 0)], 0)


def tall(x):
    return jnp.concatenate([x] * (ROWS // 8), 0)


def advect(field, rate, shift):
    magnitude = jnp.abs(rate)
    forward = rate >= 0.0
    curve = (1.0 - magnitude * magnitude) * (1.0 / 6.0)
    on_up, on_down = 0.5 + 0.5 * magnitude + 2.0 * curve, 0.5 - 0.5 * magnitude - curve
    here, ahead = tall(jnp.where(forward, on_up, on_down)), tall(jnp.where(forward, on_down, on_up))
    speed = tall(rate)
    after = shift(field, 1)
    far = jnp.where(speed >= 0.0, shift(field, -1), shift(field, 2))
    estimate = here * field + ahead * after - tall(curve) * far
    face = jnp.minimum(
        jnp.maximum(estimate, jnp.minimum(field, after)), jnp.maximum(field, after)
    )
    return field - speed * (face - shift(face, -1))


def onehot(within):
    rows = iota((GX, NB), 0).astype(f32).astype(bf16)
    return jnp.where(rows == within.astype(f32).astype(bf16), jnp.ones((), bf16), jnp.zeros((), bf16))


def two_parts(x):
    high = x.astype(bf16)
    return high, (x - high.astype(f32)).astype(bf16)


def stage_rows(b, x, lhs):
    row = jnp.concatenate([x[:GY], x[GY:]], 1)
    high, rest = two_parts(row)
    lhs[b * GY : (b + 1) * GY, :] = high
    lhs[(BINS + b) * GY : (BINS + b + 1) * GY, :] = rest


def gather_send(send, chosen, lhs, out, half):
    for c in range(HALF // 256):
        at = pl.ds(pl.multiple_of(half * HALF + c * 256, 256), 256)
        point = send[:, at]
        found = jnp.dot(lhs[...], chosen[:, at], preferred_element_type=f32)
        mine = iota((GY, 256), 0) == (point >> 8)
        rows = []
        for b in range(BINS):
            whole = found[b * GY : (b + 1) * GY] + found[(BINS + b) * GY : (BINS + b + 1) * GY]
            rows.append(jnp.sum(jnp.where(mine, whole, 0.0), axis=0, keepdims=True))
        out[:, c * 256 : (c + 1) * 256] = jnp.concatenate(rows, 0)


def grid_order(tables):
    def table(t, half):
        return tables[pl.ds(t + 4 * half, GY, stride=8), :]

    column = iota((ROWS, 128), 1) + jnp.where(iota((ROWS, 128), 0) >= GY, 128, 0)
    east = jnp.concatenate([table(0, 0), table(0, 1)], 0) & (GX - 1)
    west = jnp.concatenate([table(1, 0), table(1, 1)], 0) & (GX - 1)
    walk = jnp.where(column == 0, 0, west + GX)
    for _ in range(8):
        walk = (walk & -GX) + pick(walk, walk & (GX - 1))
    steps = walk >> 8
    reach, ring = jnp.zeros((ROWS, 128), i32), east
    for k in range(8):
        reach = jnp.where(((column >> k) & 1) == 1, pick(ring, reach), reach)
        if k < 7:
            ring = pick(ring, ring)

    north, south = table(2, 0), table(3, 0)
    upward = jnp.broadcast_to(north[0:1, 0:1], (GY, 128)) // GX == 1
    above = jnp.where(
        upward,
        jnp.broadcast_to(north[:, 0:1], (GY, 128)),
        jnp.broadcast_to(south[:, 0:1], (GY, 128)),
    ) & (GX - 1)
    above = pltpu.roll(above, 1, 0)
    within = above & 127
    offset = jnp.where(above < 128, lanes(steps[:GY], within), lanes(steps[GY:], within))
    offset = jnp.where(iota((GY, 128), 0) == 0, 0, offset)
    ladder = (iota((GY, GY), 1) <= iota((GY, GY), 0)).astype(f32).astype(bf16)
    total = jnp.dot(ladder, offset.astype(f32).astype(bf16), preferred_element_type=f32)
    start = (GX * GY - total.astype(i32)) & (GX - 1)
    start = jnp.concatenate([start, start], 0)
    order = pick(reach, (column - start) & (GX - 1))
    return order, (steps + start) & (GX - 1), jnp.where(upward[:8], 1.0, -1.0)


def packing(wet_int, windy):
    dry = (1.0 - wet_int.astype(f32)).astype(bf16)
    before = (iota((128, 128), 0) < iota((128, 128), 1)).astype(f32).astype(bf16)
    rows = jnp.dot(dry, jnp.ones((128, 128), bf16), preferred_element_type=f32)
    above_rows = (iota((ROWS, ROWS), 1) < iota((ROWS, ROWS), 0)).astype(f32).astype(bf16)
    move = jnp.dot(dry, before, preferred_element_type=f32) + jnp.dot(
        above_rows, rows.astype(bf16), preferred_element_type=f32
    )
    move = jnp.where(wet_int == 1, move.astype(i32), 0)
    lane = iota((ROWS, 128), 1)
    back_lane = lane - (move & 127)
    leave, enter = jnp.zeros((ROWS, 128), i32), jnp.zeros((ROWS, 128), i32)
    for k in range(STAGES):
        if k == LANE_STAGES:
            in_lane = lane + (move & 127)
        going = (move >> k) & 1
        other = linear_shift(move, 1 << k)
        coming = (other >> k) & 1
        leave, enter = leave | (going << k), enter | (coming << k)
        move = jnp.where(coming == 1, other, jnp.where(going == 1, 0, move))
    (windy,) = pack([windy], in_lane, enter)
    return back_lane, leave, in_lane, enter, windy[:SLOTS]


def pack(xs, in_lane, enter):
    nexts = [pltpu.roll(x, ROWS - 1, 0) for x in xs]
    xs = choose_each(xs, nexts, in_lane & 127, in_lane < 128)
    for k in range(LANE_STAGES, STAGES):
        coming = ((enter >> k) & 1) == 1
        xs = [jnp.where(coming, linear_shift(x, 1 << k), x) for x in xs]
    return xs


def unpack(xs, back_lane, leave):
    xs = [jnp.concatenate([x, x], 0) for x in xs]
    for k in reversed(range(LANE_STAGES, STAGES - 1)):
        going = ((leave >> k) & 1) == 1
        xs = [jnp.where(going, rows_unshift(x, 1 << k), x) for x in xs]
    previous = [pltpu.roll(x, 1, 0) for x in xs]
    return choose_each(xs, previous, back_lane & 127, back_lane >= 0)


def receive(incoming, recv, lhs, rhs, half):
    at = pl.ds(pl.multiple_of(half * HALF, HALF), HALF)
    row = (recv[:, at] >> 8).astype(f32).astype(bf16)
    mine = iota((GY, HALF), 0).astype(f32).astype(bf16) == row
    zero = jnp.zeros((), bf16)
    for b in range(BINS):
        high, rest = two_parts(incoming[b : b + 1, :])
        lhs[b * GY : (b + 1) * GY, :] = jnp.where(mine, jnp.broadcast_to(high, (GY, HALF)), zero)
        lhs[(BINS + b) * GY : (BINS + b + 1) * GY, :] = jnp.where(
            mine, jnp.broadcast_to(rest, (GY, HALF)), zero
        )
    lhs[2 * BINS * GY :, :] = jnp.where(mine, jnp.ones((), bf16), zero)
    return lax.dot_general(
        lhs[...], rhs[:, at], (((1,), (1,)), ((), ())), preferred_element_type=f32
    )


def substep(number, placed, field, courant, count, order, position, sea, turn):
    hit = placed[2 * BINS * GY :, :]
    hit = jnp.concatenate([hit[:, :128], hit[:, 128:]], 0) > 0.5
    scale = jnp.where(jnp.full((8, 128), count) == 2, 0.5, 1.0)
    xs = []
    for b in range(BINS):
        got = placed[b * GY : (b + 1) * GY, :] + placed[(BINS + b) * GY : (BINS + b + 1) * GY, :]
        xs.append(jnp.where(hit, jnp.concatenate([got[:, :128], got[:, 128:]], 0), field[b]))
    xs = pick_each(xs, order)
    for b in range(BINS):
        x = advect(xs[b], scale * courant[0, b], col_shift)
        xs[b] = advect(x, (scale * turn) * courant[1, b], row_shift)
    xs = pick_each(xs, position)
    if number > 0:
        still = jnp.full((ROWS, 128), count) > number
        return [jnp.where(still, x, field[b]) for b, x in enumerate(xs)]
    return [x * sea for x in xs]


def step_kernel(
    spectra, tables, wet, wind, send, recv, growth, dissipation, substeps, coupling, courant, result,
    field, lhs, wide, placed, chosen, placed_at, going, coming, packed, windy,
    columns, coarse, grown, damped, weights, back,
    weight_sem, swap_send, swap_recv, own_sem, send_sem, recv_sem, back_send, back_recv,
    plane_sem, all_sem, counted, count_sem,
):
    nest, me = lax.axis_index("nest"), lax.axis_index("bin")
    slot = lax.div(me, 4)
    y, z, x_me = lax.div(me, 32), lax.rem(slot, 8), lax.rem(me, 4)
    ys = [lax.rem(y + d, 4) for d in range(4)]
    zs = [lax.rem(z + d, 8) for d in range(8)]
    xs_at = [lax.rem(x_me + d, 4) for d in range(4)]

    def integrator(dy, dz):
        q = ys[dy] * 8 + zs[dz]
        return q, q * 4 + lax.rem(2 * nest + 32 - ys[dy] - zs[dz], 4)

    def peer(dy, dz, dx):
        return ys[dy] * 32 + zs[dz] * 4 + xs_at[dx]

    far = [0, 1, 2, 3, 4, 3, 2, 1]
    near = [0, 1, 2, 1]
    slots = sorted(
        [(dy, dz) for dy in range(4) for dz in range(8)], key=lambda d: -(near[d[0]] + far[d[1]])
    )[:-1]
    sources = sorted(
        [(dy, dz, dx) for dy in range(4) for dz in range(8) for dx in range(4)],
        key=lambda d: -(near[d[0]] + far[d[1]] + near[d[2]]),
    )[:-1]
    own_device = integrator(0, 0)[1]
    integrates = own_device == me

    def to(device):
        return {"bin": device}

    def forward(q, device):
        return pltpu.make_async_remote_copy(
            src_ref=packed.at[pl.ds(q * BINS, BINS)],
            dst_ref=columns.at[pl.ds(me * BINS, BINS)],
            send_sem=send_sem,
            recv_sem=recv_sem,
            device_id=to(device),
            device_id_type=pl.DeviceIdType.MESH,
        )

    def returning(s):
        return pltpu.make_async_remote_copy(
            src_ref=columns.at[pl.ds(s * BINS, BINS)],
            dst_ref=back.at[pl.ds(slot * BINS, BINS)],
            send_sem=back_send,
            recv_sem=back_recv,
            device_id=to(s),
            device_id_type=pl.DeviceIdType.MESH,
        )

    def several(count, ref, sent, received):
        rows = ref.at[pl.ds(0, count * BINS)]
        return pltpu.make_async_remote_copy(
            src_ref=rows,
            dst_ref=rows,
            send_sem=sent,
            recv_sem=received,
            device_id=to(lax.rem(me + 1, SOURCES)),
            device_id_type=pl.DeviceIdType.MESH,
        )

    def own_in():
        return pltpu.make_async_copy(
            packed.at[pl.ds(slot * BINS, BINS)], columns.at[pl.ds(me * BINS, BINS)], own_sem
        )

    def own_out():
        return pltpu.make_async_copy(
            columns.at[pl.ds(me * BINS, BINS)], back.at[pl.ds(slot * BINS, BINS)], own_sem
        )

    def swap(number):
        return pltpu.make_async_remote_copy(
            src_ref=going.at[number],
            dst_ref=coming.at[number],
            send_sem=swap_send.at[number],
            recv_sem=swap_recv.at[number],
            device_id={"nest": 1 - nest},
            device_id_type=pl.DeviceIdType.MESH,
        )

    def send_halves(number, start):
        def half(i, carry):
            gather_send(send, chosen, lhs, going.at[2 * number + i], i)
            if start:
                swap(2 * number + i).start()
            return carry

        lax.fori_loop(0, 2, half, 0)

    def receive_halves(number):
        def half(i, carry):
            swap(2 * number + i).wait_recv()
            placed[...] += receive(coming.at[2 * number + i], recv, wide, placed_at, i)
            return carry

        lax.fori_loop(0, 2, half, 0)

    def signal(semaphore, device):
        pl.semaphore_signal(
            semaphore, inc=1, device_id=device, device_id_type=pl.DeviceIdType.MESH
        )

    line_x = [to(peer(0, 0, d)) for d in range(1, 4)]
    line_y = [to(peer(d, 0, 0)) for d in range(1, 4)]
    line_z = [to(peer(0, d, 0)) for d in range(1, 8)]
    barrier = pltpu.get_barrier_semaphore()
    for device in line_z + line_y + line_x + [{"nest": 1 - nest}]:
        signal(barrier, device)

    fetch = pltpu.make_async_copy(coupling, weights, weight_sem)
    fetch.start()
    fetch_count = pltpu.make_async_copy(substeps, counted, count_sem)
    fetch_count.start()

    wet_int = load_split(wet)
    sea = wet_int.astype(f32)
    for b in range(BINS):
        x = load_split(spectra, b) * sea
        field[b] = x
        stage_rows(b, x, lhs)
    chosen[...] = onehot(send[...] & (GX - 1))
    placed_at[...] = onehot(recv[...] & (GX - 1))
    send_halves(0, False)
    order, position, turn = grid_order(tables)
    fetch_count.wait()
    count = counted[0]

    pl.semaphore_wait(barrier, 14)
    swap(0).start()
    swap(1).start()
    for device in line_y:
        signal(plane_sem, device)
    placed[...] = jnp.zeros_like(placed)
    for block in range(BINS):
        at = slice(block * 128, (block + 1) * 128)
        grown[at, :] = jnp.transpose(jnp.broadcast_to((SOURCE_DT * growth[at]).reshape(1, 128), (128, 128)))
        damped[at, :] = jnp.transpose(jnp.broadcast_to((SOURCE_DT * dissipation[at]).reshape(1, 128), (128, 128)))

    receive_halves(0)
    for b, x in enumerate(substep(0, placed, field, courant, count, order, position, sea, turn)):
        field[b] = x
        stage_rows(b, x, lhs)
    send_halves(1, True)
    pl.semaphore_wait(plane_sem, 3)
    for device in line_z:
        signal(all_sem, device)
    placed[...] = jnp.zeros_like(placed)
    back_lane, leave, in_lane, enter, windy[...] = packing(wet_int, load_split(wind))

    receive_halves(1)
    xs = pack(substep(1, placed, field, courant, count, order, position, sea, turn), in_lane, enter)
    for b, x in enumerate(xs):
        packed[pl.ds(b, SLOTS, stride=BINS), :] = x[:SLOTS]

    pl.semaphore_wait(all_sem, 7)
    for offset in slots:
        forward(*integrator(*offset)).start()
    fetch.wait()

    @pl.when(jnp.logical_not(integrates))
    def _():
        forward(slot, own_device).start()

    @pl.when(integrates)
    def _():
        own_in().start()
        several(SOURCES - 1, columns, send_sem, recv_sem).wait_recv()
        own_in().wait()
        blown = windy[pl.ds(slot, 1), :]

        def step(i, carry):
            v = columns[...]
            coarse[...] = v.astype(bf16)
            linear = jnp.dot(weights[...], coarse[...], preferred_element_type=f32)
            rms = jnp.sqrt(jnp.sum(v * v, axis=0, keepdims=True) * (1.0 / K) + TINY)
            columns[...] = (v + (SOURCE_DT * linear + grown[...] * blown * v)) / (
                1.0 + damped[...] * rms
            )
            return carry

        lax.fori_loop(0, SRC, step, 0)
        for offset in sources:
            returning(peer(*offset)).start()
        own_out().start()
        own_out().wait()
        several(SLOTS - 1, back, back_send, back_recv).wait_recv()

    @pl.when(jnp.logical_not(integrates))
    def _():
        several(SLOTS, back, back_send, back_recv).wait_recv()

    xs = unpack(
        [back[pl.ds(b, SLOTS, stride=BINS), :] for b in range(BINS)], back_lane, leave
    )
    for b, x in enumerate(xs):
        for half in range(2):
            result[b, pl.ds(half, GY, stride=2), :] = x[half * GY : (half + 1) * GY]

    for number in range(2 * SUBSTEPS):
        swap(number).wait_send()

    @pl.when(integrates)
    def _():
        several(SLOTS - 1, packed, send_sem, recv_sem).wait_send()
        several(SOURCES - 1, columns, back_send, back_recv).wait_send()

    @pl.when(jnp.logical_not(integrates))
    def _():
        several(SLOTS, packed, send_sem, recv_sem).wait_send()


def local(
    spectra, courant, coupling, growth, dissipation, wind,
    neighbours, wet_mask, send_list, recv_list, substep_count,
):
    plane = (ROWS, 128)
    tables = neighbours.reshape(4, ROWS, 128).transpose(1, 0, 2).reshape(4 * ROWS, 128)
    vmem = pl.BlockSpec(memory_space=pltpu.VMEM)
    smem = pl.BlockSpec(memory_space=pltpu.SMEM)
    result = pl.pallas_call(
        step_kernel,
        out_shape=pltpu.VMEM((BINS, ROWS, 128), f32),
        in_specs=[vmem] * 8 + [pl.BlockSpec(memory_space=pl.ANY)] * 2 + [smem],
        out_specs=vmem,
        scratch_shapes=[
            pltpu.VMEM((BINS, ROWS, 128), f32),
            pltpu.VMEM((2 * BINS * GY, GX), bf16),
            pltpu.VMEM((2 * BINS * GY + GY, HALF), bf16),
            pltpu.VMEM((2 * BINS * GY + GY, GX), f32),
            pltpu.VMEM((GX, NB), bf16),
            pltpu.VMEM((GX, NB), bf16),
            pltpu.VMEM((2 * SUBSTEPS, BINS, HALF), f32),
            pltpu.VMEM((2 * SUBSTEPS, BINS, HALF), f32),
            pltpu.VMEM((SLOTS * BINS, 128), f32),
            pltpu.VMEM((SLOTS, 128), f32),
            pltpu.VMEM((K, 128), f32),
            pltpu.VMEM((K, 128), bf16),
            pltpu.VMEM((K, 128), f32),
            pltpu.VMEM((K, 128), f32),
            pltpu.VMEM((K, K), bf16),
            pltpu.VMEM((SLOTS * BINS, 128), f32),
            pltpu.SemaphoreType.DMA,
            pltpu.SemaphoreType.DMA((2 * SUBSTEPS,)),
            pltpu.SemaphoreType.DMA((2 * SUBSTEPS,)),
            pltpu.SemaphoreType.DMA,
            pltpu.SemaphoreType.DMA,
            pltpu.SemaphoreType.DMA,
            pltpu.SemaphoreType.DMA,
            pltpu.SemaphoreType.DMA,
            pltpu.SemaphoreType.REGULAR,
            pltpu.SemaphoreType.REGULAR,
            pltpu.SMEM((1,), i32),
            pltpu.SemaphoreType.DMA,
        ],
        compiler_params=pltpu.CompilerParams(collective_id=0, has_side_effects=True),
    )(
        spectra.reshape(BINS, ROWS, 128), tables, wet_mask.reshape(plane), wind.reshape(plane),
        send_list, recv_list, growth, dissipation,
        substep_count, coupling, courant,
    )
    result = jnp.where(wet_mask.reshape(plane)[None] == 1, result, 0.0)
    return result.reshape(1, BINS, ROWS * 128)


def solution(mesh):
    in_specs = (
        P("nest", "bin", None), P(None, "bin"), P(), P(), P(), P("nest", None),
        P("nest", None, None), P("nest", None), P("nest", None), P("nest", None), P("nest"),
    )
    return jax.shard_map(
        local, mesh=mesh, in_specs=in_specs, out_specs=P("nest", "bin", None), check_vma=False
    )
```

```python
import jax
import jax.numpy as jnp
from jax import lax
from jax.experimental import pallas as pl
from jax.experimental.pallas import tpu as pltpu
from jax.sharding import PartitionSpec as P

SUBSTEPS = 2
SRC = 5
SOURCE_DT = 0.25
TINY = 1e-06
GX = 256
GY = 32
BINS = 9
K = 1152
ROWS = 64
NB = 2048
HALF = 1024
SLOTS = 32
SOURCES = 128
STAGES = 13
LANE_STAGES = 7
f32, bf16, i32 = jnp.float32, jnp.bfloat16, jnp.int32


def iota(shape, dim):
    return lax.broadcasted_iota(i32, shape, dim)


def lanes(x, index):
    return jnp.take_along_axis(x, index, axis=1, mode="promise_in_bounds")


def pick(table, index):
    low = jnp.concatenate([table[:GY], table[:GY]], 0)
    high = jnp.concatenate([table[GY:], table[GY:]], 0)
    within = index & 127
    return jnp.where(index < 128, lanes(low, within), lanes(high, within))


def load_split(ref, *lead):
    return jnp.concatenate(
        [ref[(*lead, pl.ds(half, GY, stride=2), slice(None))] for half in range(2)], 0
    )


def linear_shift(x, amount):
    if amount >= 128:
        return pltpu.roll(x, ROWS - amount // 128, 0)
    turned = pltpu.roll(x, 128 - amount, 1)
    return jnp.where(iota(x.shape, 1) >= 128 - amount, pltpu.roll(turned, ROWS - 1, 0), turned)


def rows_unshift(x, amount):
    return pltpu.roll(x, amount // 128, 0)


def choose_each(firsts, seconds, lane, use_first):
    parts = [[] for _ in firsts]
    for at in range(0, ROWS, 8):
        low = at % firsts[0].shape[0]
        within, mask = lane[at : at + 8], use_first[at : at + 8]
        for part, first, second in zip(parts, firsts, seconds):
            part.append(
                jnp.where(mask, lanes(first[low : low + 8], within), lanes(second[low : low + 8], within))
            )
    return [jnp.concatenate(part, 0) for part in parts]


def pick_each(tables, index):
    return choose_each(
        [table[:GY] for table in tables], [table[GY:] for table in tables], index & 127, index < 128
    )


def col_shift(x, amount):
    lane = iota((GY, 128), 1)
    low = pltpu.roll(x[:GY], (128 - amount) % 128, 1)
    high = pltpu.roll(x[GY:], (128 - amount) % 128, 1)
    crossed = lane >= 128 - amount if amount > 0 else lane < -amount
    return jnp.concatenate([jnp.where(crossed, high, low), jnp.where(crossed, low, high)], 0)


def row_shift(x, amount):
    turn = (GY - amount) % GY
    return jnp.concatenate([pltpu.roll(x[:GY], turn, 0), pltpu.roll(x[GY:], turn, 0)], 0)


def tall(x):
    return jnp.concatenate([x] * (ROWS // 8), 0)


def advect(field, rate, shift):
    magnitude = jnp.abs(rate)
    forward = rate >= 0.0
    curve = (1.0 - magnitude * magnitude) * (1.0 / 6.0)
    on_up, on_down = 0.5 + 0.5 * magnitude + 2.0 * curve, 0.5 - 0.5 * magnitude - curve
    here, ahead = tall(jnp.where(forward, on_up, on_down)), tall(jnp.where(forward, on_down, on_up))
    speed = tall(rate)
    after = shift(field, 1)
    far = jnp.where(speed >= 0.0, shift(field, -1), shift(field, 2))
    estimate = here * field + ahead * after - tall(curve) * far
    face = jnp.minimum(
        jnp.maximum(estimate, jnp.minimum(field, after)), jnp.maximum(field, after)
    )
    return field - speed * (face - shift(face, -1))


def onehot(within):
    rows = iota((GX, NB), 0).astype(f32).astype(bf16)
    return jnp.where(rows == within.astype(f32).astype(bf16), jnp.ones((), bf16), jnp.zeros((), bf16))


def two_parts(x):
    high = x.astype(bf16)
    return high, (x - high.astype(f32)).astype(bf16)


def stage_rows(b, x, lhs):
    row = jnp.concatenate([x[:GY], x[GY:]], 1)
    high, rest = two_parts(row)
    lhs[b * GY : (b + 1) * GY, :] = high
    lhs[(BINS + b) * GY : (BINS + b + 1) * GY, :] = rest


def gather_send(send, chosen, lhs, out, half):
    for c in range(HALF // 256):
        at = pl.ds(pl.multiple_of(half * HALF + c * 256, 256), 256)
        point = send[:, at]
        found = jnp.dot(lhs[...], chosen[:, at], preferred_element_type=f32)
        mine = iota((GY, 256), 0) == (point >> 8)
        rows = []
        for b in range(BINS):
            whole = found[b * GY : (b + 1) * GY] + found[(BINS + b) * GY : (BINS + b + 1) * GY]
            rows.append(jnp.sum(jnp.where(mine, whole, 0.0), axis=0, keepdims=True))
        out[:, c * 256 : (c + 1) * 256] = jnp.concatenate(rows, 0)


def grid_order(tables):
    def table(t, half):
        return tables[pl.ds(t + 4 * half, GY, stride=8), :]

    column = iota((ROWS, 128), 1) + jnp.where(iota((ROWS, 128), 0) >= GY, 128, 0)
    east = jnp.concatenate([table(0, 0), table(0, 1)], 0) & (GX - 1)
    west = jnp.concatenate([table(1, 0), table(1, 1)], 0) & (GX - 1)
    walk = jnp.where(column == 0, 0, west + GX)
    for _ in range(8):
        walk = (walk & -GX) + pick(walk, walk & (GX - 1))
    steps = walk >> 8
    reach, ring = jnp.zeros((ROWS, 128), i32), east
    for k in range(8):
        reach = jnp.where(((column >> k) & 1) == 1, pick(ring, reach), reach)
        if k < 7:
            ring = pick(ring, ring)

    north, south = table(2, 0), table(3, 0)
    upward = jnp.broadcast_to(north[0:1, 0:1], (GY, 128)) // GX == 1
    above = jnp.where(
        upward,
        jnp.broadcast_to(north[:, 0:1], (GY, 128)),
        jnp.broadcast_to(south[:, 0:1], (GY, 128)),
    ) & (GX - 1)
    above = pltpu.roll(above, 1, 0)
    within = above & 127
    offset = jnp.where(above < 128, lanes(steps[:GY], within), lanes(steps[GY:], within))
    offset = jnp.where(iota((GY, 128), 0) == 0, 0, offset)
    ladder = (iota((GY, GY), 1) <= iota((GY, GY), 0)).astype(f32).astype(bf16)
    total = jnp.dot(ladder, offset.astype(f32).astype(bf16), preferred_element_type=f32)
    start = (GX * GY - total.astype(i32)) & (GX - 1)
    start = jnp.concatenate([start, start], 0)
    order = pick(reach, (column - start) & (GX - 1))
    return order, (steps + start) & (GX - 1), jnp.where(upward[:8], 1.0, -1.0)


def packing(wet_int, windy):
    dry = (1.0 - wet_int.astype(f32)).astype(bf16)
    before = (iota((128, 128), 0) < iota((128, 128), 1)).astype(f32).astype(bf16)
    rows = jnp.dot(dry, jnp.ones((128, 128), bf16), preferred_element_type=f32)
    above_rows = (iota((ROWS, ROWS), 1) < iota((ROWS, ROWS), 0)).astype(f32).astype(bf16)
    move = jnp.dot(dry, before, preferred_element_type=f32) + jnp.dot(
        above_rows, rows.astype(bf16), preferred_element_type=f32
    )
    move = jnp.where(wet_int == 1, move.astype(i32), 0)
    lane = iota((ROWS, 128), 1)
    back_lane = lane - (move & 127)
    leave, enter = jnp.zeros((ROWS, 128), i32), jnp.zeros((ROWS, 128), i32)
    for k in range(STAGES):
        if k == LANE_STAGES:
            in_lane = lane + (move & 127)
        going = (move >> k) & 1
        other = linear_shift(move, 1 << k)
        coming = (other >> k) & 1
        leave, enter = leave | (going << k), enter | (coming << k)
        move = jnp.where(coming == 1, other, jnp.where(going == 1, 0, move))
    (windy,) = pack([windy], in_lane, enter)
    return back_lane, leave, in_lane, enter, windy[:SLOTS]


def pack(xs, in_lane, enter):
    nexts = [pltpu.roll(x, ROWS - 1, 0) for x in xs]
    xs = choose_each(xs, nexts, in_lane & 127, in_lane < 128)
    for k in range(LANE_STAGES, STAGES):
        coming = ((enter >> k) & 1) == 1
        xs = [jnp.where(coming, linear_shift(x, 1 << k), x) for x in xs]
    return xs


def unpack(xs, back_lane, leave):
    xs = [jnp.concatenate([x, x], 0) for x in xs]
    for k in reversed(range(LANE_STAGES, STAGES - 1)):
        going = ((leave >> k) & 1) == 1
        xs = [jnp.where(going, rows_unshift(x, 1 << k), x) for x in xs]
    previous = [pltpu.roll(x, 1, 0) for x in xs]
    return choose_each(xs, previous, back_lane & 127, back_lane >= 0)


def receive(incoming, recv, lhs, rhs):
    row = (recv[...] >> 8).astype(f32).astype(bf16)
    mine = iota((GY, NB), 0).astype(f32).astype(bf16) == row
    zero = jnp.zeros((), bf16)
    for b in range(BINS):
        value = jnp.concatenate([incoming[half, b : b + 1, :] for half in range(2)], 1)
        high, rest = two_parts(value)
        lhs[b * GY : (b + 1) * GY, :] = jnp.where(mine, jnp.broadcast_to(high, (GY, NB)), zero)
        lhs[(BINS + b) * GY : (BINS + b + 1) * GY, :] = jnp.where(
            mine, jnp.broadcast_to(rest, (GY, NB)), zero
        )
    lhs[2 * BINS * GY :, :] = jnp.where(mine, jnp.ones((), bf16), zero)
    return lax.dot_general(
        lhs[...], rhs[...], (((1,), (1,)), ((), ())), preferred_element_type=f32
    )


def substep(number, placed, field, courant, count, order, position, sea, turn):
    hit = placed[2 * BINS * GY :, :]
    hit = jnp.concatenate([hit[:, :128], hit[:, 128:]], 0) > 0.5
    scale = jnp.where(jnp.full((8, 128), count) == 2, 0.5, 1.0)
    xs = []
    for b in range(BINS):
        got = placed[b * GY : (b + 1) * GY, :] + placed[(BINS + b) * GY : (BINS + b + 1) * GY, :]
        xs.append(jnp.where(hit, jnp.concatenate([got[:, :128], got[:, 128:]], 0), field[b]))
    xs = pick_each(xs, order)
    for b in range(BINS):
        x = advect(xs[b], scale * courant[0, b], col_shift)
        xs[b] = advect(x, (scale * turn) * courant[1, b], row_shift)
    xs = pick_each(xs, position)
    if number > 0:
        still = jnp.full((ROWS, 128), count) > number
        return [jnp.where(still, x, field[b]) for b, x in enumerate(xs)]
    return [x * sea for x in xs]


def step_kernel(
    spectra, tables, wet, wind, send, recv, growth, dissipation, substeps, coupling, courant, result,
    field, lhs, wide, chosen, placed_at, going, coming, packed, windy,
    columns, coarse, grown, damped, weights, back,
    weight_sem, swap_send, swap_recv, own_sem, send_sem, recv_sem, back_send, back_recv,
    plane_sem, all_sem, counted, count_sem,
):
    nest, me = lax.axis_index("nest"), lax.axis_index("bin")
    slot = lax.div(me, 4)
    y, z, x_me = lax.div(me, 32), lax.rem(slot, 8), lax.rem(me, 4)
    ys = [lax.rem(y + d, 4) for d in range(4)]
    zs = [lax.rem(z + d, 8) for d in range(8)]
    xs_at = [lax.rem(x_me + d, 4) for d in range(4)]

    def integrator(dy, dz):
        q = ys[dy] * 8 + zs[dz]
        return q, q * 4 + lax.rem(2 * nest + 32 - ys[dy] - zs[dz], 4)

    def peer(dy, dz, dx):
        return ys[dy] * 32 + zs[dz] * 4 + xs_at[dx]

    far = [0, 1, 2, 3, 4, 3, 2, 1]
    near = [0, 1, 2, 1]
    slots = sorted(
        [(dy, dz) for dy in range(4) for dz in range(8)], key=lambda d: -(near[d[0]] + far[d[1]])
    )[:-1]
    sources = sorted(
        [(dy, dz, dx) for dy in range(4) for dz in range(8) for dx in range(4)],
        key=lambda d: -(near[d[0]] + far[d[1]] + near[d[2]]),
    )[:-1]
    own_device = integrator(0, 0)[1]
    integrates = own_device == me

    def to(device):
        return {"bin": device}

    def forward(q, device):
        return pltpu.make_async_remote_copy(
            src_ref=packed.at[pl.ds(q * BINS, BINS)],
            dst_ref=columns.at[pl.ds(me * BINS, BINS)],
            send_sem=send_sem,
            recv_sem=recv_sem,
            device_id=to(device),
            device_id_type=pl.DeviceIdType.MESH,
        )

    def returning(s):
        return pltpu.make_async_remote_copy(
            src_ref=columns.at[pl.ds(s * BINS, BINS)],
            dst_ref=back.at[pl.ds(slot * BINS, BINS)],
            send_sem=back_send,
            recv_sem=back_recv,
            device_id=to(s),
            device_id_type=pl.DeviceIdType.MESH,
        )

    def several(count, ref, sent, received):
        rows = ref.at[pl.ds(0, count * BINS)]
        return pltpu.make_async_remote_copy(
            src_ref=rows,
            dst_ref=rows,
            send_sem=sent,
            recv_sem=received,
            device_id=to(lax.rem(me + 1, SOURCES)),
            device_id_type=pl.DeviceIdType.MESH,
        )

    def own_in():
        return pltpu.make_async_copy(
            packed.at[pl.ds(slot * BINS, BINS)], columns.at[pl.ds(me * BINS, BINS)], own_sem
        )

    def own_out():
        return pltpu.make_async_copy(
            columns.at[pl.ds(me * BINS, BINS)], back.at[pl.ds(slot * BINS, BINS)], own_sem
        )

    def swap(number):
        return pltpu.make_async_remote_copy(
            src_ref=going.at[number],
            dst_ref=coming.at[number],
            send_sem=swap_send.at[number],
            recv_sem=swap_recv.at[number],
            device_id={"nest": 1 - nest},
            device_id_type=pl.DeviceIdType.MESH,
        )

    def send_halves(number, start):
        def half(i, carry):
            gather_send(send, chosen, lhs, going.at[2 * number + i], i)
            if start:
                swap(2 * number + i).start()
            return carry

        lax.fori_loop(0, 2, half, 0)

    def receive_halves(number):
        for half in range(2):
            swap(2 * number + half).wait_recv()
        return receive(coming.at[2 * number : 2 * number + 2], recv, wide, placed_at)

    def signal(semaphore, device):
        pl.semaphore_signal(
            semaphore, inc=1, device_id=device, device_id_type=pl.DeviceIdType.MESH
        )

    line_x = [to(peer(0, 0, d)) for d in range(1, 4)]
    line_y = [to(peer(d, 0, 0)) for d in range(1, 4)]
    line_z = [to(peer(0, d, 0)) for d in range(1, 8)]
    barrier = pltpu.get_barrier_semaphore()
    for device in line_z + line_y + line_x + [{"nest": 1 - nest}]:
        signal(barrier, device)

    fetch = pltpu.make_async_copy(coupling, weights, weight_sem)
    fetch.start()
    fetch_count = pltpu.make_async_copy(substeps, counted, count_sem)
    fetch_count.start()

    wet_int = load_split(wet)
    sea = wet_int.astype(f32)
    for b in range(BINS):
        x = load_split(spectra, b) * sea
        field[b] = x
        stage_rows(b, x, lhs)
    chosen[...] = onehot(send[...] & (GX - 1))
    placed_at[...] = onehot(recv[...] & (GX - 1))
    send_halves(0, False)
    order, position, turn = grid_order(tables)
    fetch_count.wait()
    count = counted[0]

    pl.semaphore_wait(barrier, 14)
    swap(0).start()
    swap(1).start()
    for device in line_y:
        signal(plane_sem, device)
    for block in range(BINS):
        at = slice(block * 128, (block + 1) * 128)
        grown[at, :] = jnp.transpose(jnp.broadcast_to((SOURCE_DT * growth[at]).reshape(1, 128), (128, 128)))
        damped[at, :] = jnp.transpose(jnp.broadcast_to((SOURCE_DT * dissipation[at]).reshape(1, 128), (128, 128)))

    placed = receive_halves(0)
    for b, x in enumerate(substep(0, placed, field, courant, count, order, position, sea, turn)):
        field[b] = x
        stage_rows(b, x, lhs)
    send_halves(1, True)
    pl.semaphore_wait(plane_sem, 3)
    for device in line_z:
        signal(all_sem, device)
    back_lane, leave, in_lane, enter, windy[...] = packing(wet_int, load_split(wind))

    placed = receive_halves(1)
    xs = pack(substep(1, placed, field, courant, count, order, position, sea, turn), in_lane, enter)
    for b, x in enumerate(xs):
        packed[pl.ds(b, SLOTS, stride=BINS), :] = x[:SLOTS]

    pl.semaphore_wait(all_sem, 7)
    for offset in slots:
        forward(*integrator(*offset)).start()
    fetch.wait()

    @pl.when(jnp.logical_not(integrates))
    def _():
        forward(slot, own_device).start()

    @pl.when(integrates)
    def _():
        own_in().start()
        several(SOURCES - 1, columns, send_sem, recv_sem).wait_recv()
        own_in().wait()
        blown = windy[pl.ds(slot, 1), :]

        def step(i, carry):
            v = columns[...]
            coarse[...] = v.astype(bf16)
            linear = jnp.dot(weights[...], coarse[...], preferred_element_type=f32)
            rms = jnp.sqrt(jnp.sum(v * v, axis=0, keepdims=True) * (1.0 / K) + TINY)
            columns[...] = (v + (SOURCE_DT * linear + grown[...] * blown * v)) / (
                1.0 + damped[...] * rms
            )
            return carry

        lax.fori_loop(0, SRC, step, 0)
        for offset in sources:
            returning(peer(*offset)).start()
        own_out().start()
        own_out().wait()
        several(SLOTS - 1, back, back_send, back_recv).wait_recv()

    @pl.when(jnp.logical_not(integrates))
    def _():
        several(SLOTS, back, back_send, back_recv).wait_recv()

    xs = unpack(
        [back[pl.ds(b, SLOTS, stride=BINS), :] for b in range(BINS)], back_lane, leave
    )
    for b, x in enumerate(xs):
        for half in range(2):
            result[b, pl.ds(half, GY, stride=2), :] = x[half * GY : (half + 1) * GY]

    for number in range(2 * SUBSTEPS):
        swap(number).wait_send()

    @pl.when(integrates)
    def _():
        several(SLOTS - 1, packed, send_sem, recv_sem).wait_send()
        several(SOURCES - 1, columns, back_send, back_recv).wait_send()

    @pl.when(jnp.logical_not(integrates))
    def _():
        several(SLOTS, packed, send_sem, recv_sem).wait_send()


def local(
    spectra, courant, coupling, growth, dissipation, wind,
    neighbours, wet_mask, send_list, recv_list, substep_count,
):
    plane = (ROWS, 128)
    tables = neighbours.reshape(4, ROWS, 128).transpose(1, 0, 2).reshape(4 * ROWS, 128)
    vmem = pl.BlockSpec(memory_space=pltpu.VMEM)
    smem = pl.BlockSpec(memory_space=pltpu.SMEM)
    result = pl.pallas_call(
        step_kernel,
        out_shape=pltpu.VMEM((BINS, ROWS, 128), f32),
        in_specs=[vmem] * 8 + [pl.BlockSpec(memory_space=pl.ANY)] * 2 + [smem],
        out_specs=vmem,
        scratch_shapes=[
            pltpu.VMEM((BINS, ROWS, 128), f32),
            pltpu.VMEM((2 * BINS * GY, GX), bf16),
            pltpu.VMEM((2 * BINS * GY + GY, NB), bf16),
            pltpu.VMEM((GX, NB), bf16),
            pltpu.VMEM((GX, NB), bf16),
            pltpu.VMEM((2 * SUBSTEPS, BINS, HALF), f32),
            pltpu.VMEM((2 * SUBSTEPS, BINS, HALF), f32),
            pltpu.VMEM((SLOTS * BINS, 128), f32),
            pltpu.VMEM((SLOTS, 128), f32),
            pltpu.VMEM((K, 128), f32),
            pltpu.VMEM((K, 128), bf16),
            pltpu.VMEM((K, 128), f32),
            pltpu.VMEM((K, 128), f32),
            pltpu.VMEM((K, K), bf16),
            pltpu.VMEM((SLOTS * BINS, 128), f32),
            pltpu.SemaphoreType.DMA,
            pltpu.SemaphoreType.DMA((2 * SUBSTEPS,)),
            pltpu.SemaphoreType.DMA((2 * SUBSTEPS,)),
            pltpu.SemaphoreType.DMA,
            pltpu.SemaphoreType.DMA,
            pltpu.SemaphoreType.DMA,
            pltpu.SemaphoreType.DMA,
            pltpu.SemaphoreType.DMA,
            pltpu.SemaphoreType.REGULAR,
            pltpu.SemaphoreType.REGULAR,
            pltpu.SMEM((1,), i32),
            pltpu.SemaphoreType.DMA,
        ],
        compiler_params=pltpu.CompilerParams(collective_id=0, has_side_effects=True),
    )(
        spectra.reshape(BINS, ROWS, 128), tables, wet_mask.reshape(plane), wind.reshape(plane),
        send_list, recv_list, growth, dissipation,
        substep_count, coupling, courant,
    )
    result = jnp.where(wet_mask.reshape(plane)[None] == 1, result, 0.0)
    return result.reshape(1, BINS, ROWS * 128)


def solution(mesh):
    in_specs = (
        P("nest", "bin", None), P(None, "bin"), P(), P(), P(), P("nest", None),
        P("nest", None, None), P("nest", None), P("nest", None), P("nest", None), P("nest"),
    )
    return jax.shard_map(
        local, mesh=mesh, in_specs=in_specs, out_specs=P("nest", "bin", None), check_vma=False
    )
```

```python
import jax
import jax.numpy as jnp
from jax import lax
from jax.experimental import pallas as pl
from jax.experimental.pallas import tpu as pltpu
from jax.sharding import PartitionSpec as P

SUBSTEPS = 2
SRC = 5
SOURCE_DT = 0.25
TINY = 1e-06
GX = 256
GY = 32
BINS = 9
K = 1152
ROWS = 64
NB = 2048
HALF = 1024
SLOTS = 32
SOURCES = 128
STAGES = 13
LANE_STAGES = 7
f32, bf16, i32 = jnp.float32, jnp.bfloat16, jnp.int32


def iota(shape, dim):
    return lax.broadcasted_iota(i32, shape, dim)


def lanes(x, index):
    return jnp.take_along_axis(x, index, axis=1, mode="promise_in_bounds")


def pick(table, index):
    low = jnp.concatenate([table[:GY], table[:GY]], 0)
    high = jnp.concatenate([table[GY:], table[GY:]], 0)
    within = index & 127
    return jnp.where(index < 128, lanes(low, within), lanes(high, within))


def load_split(ref, *lead):
    return jnp.concatenate(
        [ref[(*lead, pl.ds(half, GY, stride=2), slice(None))] for half in range(2)], 0
    )


def linear_shift(x, amount):
    if amount >= 128:
        return pltpu.roll(x, ROWS - amount // 128, 0)
    turned = pltpu.roll(x, 128 - amount, 1)
    return jnp.where(iota(x.shape, 1) >= 128 - amount, pltpu.roll(turned, ROWS - 1, 0), turned)


def rows_unshift(x, amount):
    return pltpu.roll(x, amount // 128, 0)


def choose_each(firsts, seconds, lane, use_first):
    parts = [[] for _ in firsts]
    for at in range(0, ROWS, 8):
        low = at % firsts[0].shape[0]
        within, mask = lane[at : at + 8], use_first[at : at + 8]
        for part, first, second in zip(parts, firsts, seconds):
            part.append(
                jnp.where(mask, lanes(first[low : low + 8], within), lanes(second[low : low + 8], within))
            )
    return [jnp.concatenate(part, 0) for part in parts]


def pick_each(tables, index):
    return choose_each(
        [table[:GY] for table in tables], [table[GY:] for table in tables], index & 127, index < 128
    )


def col_shift(x, amount):
    lane = iota((GY, 128), 1)
    low = pltpu.roll(x[:GY], (128 - amount) % 128, 1)
    high = pltpu.roll(x[GY:], (128 - amount) % 128, 1)
    crossed = lane >= 128 - amount if amount > 0 else lane < -amount
    return jnp.concatenate([jnp.where(crossed, high, low), jnp.where(crossed, low, high)], 0)


def row_shift(x, amount):
    turn = (GY - amount) % GY
    return jnp.concatenate([pltpu.roll(x[:GY], turn, 0), pltpu.roll(x[GY:], turn, 0)], 0)


def tall(x):
    return jnp.concatenate([x] * (ROWS // 8), 0)


def advect(field, rate, shift):
    magnitude = jnp.abs(rate)
    forward = rate >= 0.0
    curve = (1.0 - magnitude * magnitude) * (1.0 / 6.0)
    on_up, on_down = 0.5 + 0.5 * magnitude + 2.0 * curve, 0.5 - 0.5 * magnitude - curve
    here, ahead = tall(jnp.where(forward, on_up, on_down)), tall(jnp.where(forward, on_down, on_up))
    speed = tall(rate)
    after = shift(field, 1)
    far = jnp.where(speed >= 0.0, shift(field, -1), shift(field, 2))
    estimate = here * field + ahead * after - tall(curve) * far
    face = jnp.minimum(
        jnp.maximum(estimate, jnp.minimum(field, after)), jnp.maximum(field, after)
    )
    return field - speed * (face - shift(face, -1))


def onehot(within):
    rows = iota((GX, NB), 0).astype(f32).astype(bf16)
    return jnp.where(rows == within.astype(f32).astype(bf16), jnp.ones((), bf16), jnp.zeros((), bf16))


def two_parts(x):
    high = x.astype(bf16)
    return high, (x - high.astype(f32)).astype(bf16)


def stage_rows(b, x, lhs):
    row = jnp.concatenate([x[:GY], x[GY:]], 1)
    high, rest = two_parts(row)
    lhs[b * GY : (b + 1) * GY, :] = high
    lhs[(BINS + b) * GY : (BINS + b + 1) * GY, :] = rest


def gather_send(send, chosen, lhs, out, half):
    for c in range(HALF // 256):
        at = pl.ds(pl.multiple_of(half * HALF + c * 256, 256), 256)
        point = send[:, at]
        found = jnp.dot(lhs[...], chosen[:, at], preferred_element_type=f32)
        mine = iota((GY, 256), 0) == (point >> 8)
        rows = []
        for b in range(BINS):
            whole = found[b * GY : (b + 1) * GY] + found[(BINS + b) * GY : (BINS + b + 1) * GY]
            rows.append(jnp.sum(jnp.where(mine, whole, 0.0), axis=0, keepdims=True))
        out[:, c * 256 : (c + 1) * 256] = jnp.concatenate(rows, 0)


def grid_order(tables):
    def table(t, half):
        return tables[pl.ds(t + 4 * half, GY, stride=8), :]

    column = iota((ROWS, 128), 1) + jnp.where(iota((ROWS, 128), 0) >= GY, 128, 0)
    east = jnp.concatenate([table(0, 0), table(0, 1)], 0) & (GX - 1)
    west = jnp.concatenate([table(1, 0), table(1, 1)], 0) & (GX - 1)
    walk = jnp.where(column == 0, 0, west + GX)
    for _ in range(8):
        walk = (walk & -GX) + pick(walk, walk & (GX - 1))
    steps = walk >> 8
    reach, ring = jnp.zeros((ROWS, 128), i32), east
    for k in range(8):
        reach = jnp.where(((column >> k) & 1) == 1, pick(ring, reach), reach)
        if k < 7:
            ring = pick(ring, ring)

    north, south = table(2, 0), table(3, 0)
    upward = jnp.broadcast_to(north[0:1, 0:1], (GY, 128)) // GX == 1
    above = jnp.where(
        upward,
        jnp.broadcast_to(north[:, 0:1], (GY, 128)),
        jnp.broadcast_to(south[:, 0:1], (GY, 128)),
    ) & (GX - 1)
    above = pltpu.roll(above, 1, 0)
    within = above & 127
    offset = jnp.where(above < 128, lanes(steps[:GY], within), lanes(steps[GY:], within))
    offset = jnp.where(iota((GY, 128), 0) == 0, 0, offset)
    ladder = (iota((GY, GY), 1) <= iota((GY, GY), 0)).astype(f32).astype(bf16)
    total = jnp.dot(ladder, offset.astype(f32).astype(bf16), preferred_element_type=f32)
    start = (GX * GY - total.astype(i32)) & (GX - 1)
    start = jnp.concatenate([start, start], 0)
    order = pick(reach, (column - start) & (GX - 1))
    return order, (steps + start) & (GX - 1), jnp.where(upward[:8], 1.0, -1.0)


def packing(wet_int, windy):
    dry = (1.0 - wet_int.astype(f32)).astype(bf16)
    before = (iota((128, 128), 0) < iota((128, 128), 1)).astype(f32).astype(bf16)
    rows = jnp.dot(dry, jnp.ones((128, 128), bf16), preferred_element_type=f32)
    above_rows = (iota((ROWS, ROWS), 1) < iota((ROWS, ROWS), 0)).astype(f32).astype(bf16)
    move = jnp.dot(dry, before, preferred_element_type=f32) + jnp.dot(
        above_rows, rows.astype(bf16), preferred_element_type=f32
    )
    move = jnp.where(wet_int == 1, move.astype(i32), 0)
    lane = iota((ROWS, 128), 1)
    back_lane = lane - (move & 127)
    leave, enter = jnp.zeros((ROWS, 128), i32), jnp.zeros((ROWS, 128), i32)
    for k in range(STAGES):
        if k == LANE_STAGES:
            in_lane = lane + (move & 127)
        going = (move >> k) & 1
        other = linear_shift(move, 1 << k)
        coming = (other >> k) & 1
        leave, enter = leave | (going << k), enter | (coming << k)
        move = jnp.where(coming == 1, other, jnp.where(going == 1, 0, move))
    (windy,) = pack([windy], in_lane, enter)
    return back_lane, leave, in_lane, enter, windy[:SLOTS]


def pack(xs, in_lane, enter):
    nexts = [pltpu.roll(x, ROWS - 1, 0) for x in xs]
    xs = choose_each(xs, nexts, in_lane & 127, in_lane < 128)
    for k in range(LANE_STAGES, STAGES):
        coming = ((enter >> k) & 1) == 1
        xs = [jnp.where(coming, linear_shift(x, 1 << k), x) for x in xs]
    return xs


def unpack(xs, back_lane, leave):
    xs = [jnp.concatenate([x, x], 0) for x in xs]
    for k in reversed(range(LANE_STAGES, STAGES - 1)):
        going = ((leave >> k) & 1) == 1
        xs = [jnp.where(going, rows_unshift(x, 1 << k), x) for x in xs]
    previous = [pltpu.roll(x, 1, 0) for x in xs]
    return choose_each(xs, previous, back_lane & 127, back_lane >= 0)


def receive(incoming, recv, lhs, rhs):
    row = (recv[...] >> 8).astype(f32).astype(bf16)
    mine = iota((GY, NB), 0).astype(f32).astype(bf16) == row
    zero = jnp.zeros((), bf16)
    for b in range(BINS):
        value = jnp.concatenate([incoming[half, b : b + 1, :] for half in range(2)], 1)
        high, rest = two_parts(value)
        lhs[b * GY : (b + 1) * GY, :] = jnp.where(mine, jnp.broadcast_to(high, (GY, NB)), zero)
        lhs[(BINS + b) * GY : (BINS + b + 1) * GY, :] = jnp.where(
            mine, jnp.broadcast_to(rest, (GY, NB)), zero
        )
    lhs[2 * BINS * GY :, :] = jnp.where(mine, jnp.ones((), bf16), zero)
    return lax.dot_general(
        lhs[...], rhs[...], (((1,), (1,)), ((), ())), preferred_element_type=f32
    )


def substep(number, placed, field, courant, count, order, position, sea, turn):
    hit = placed[2 * BINS * GY :, :]
    hit = jnp.concatenate([hit[:, :128], hit[:, 128:]], 0) > 0.5
    scale = jnp.where(jnp.full((8, 128), count) == 2, 0.5, 1.0)
    xs = []
    for b in range(BINS):
        got = placed[b * GY : (b + 1) * GY, :] + placed[(BINS + b) * GY : (BINS + b + 1) * GY, :]
        xs.append(jnp.where(hit, jnp.concatenate([got[:, :128], got[:, 128:]], 0), field[b]))
    xs = pick_each(xs, order)
    for b in range(BINS):
        x = advect(xs[b], scale * courant[0, b], col_shift)
        xs[b] = advect(x, (scale * turn) * courant[1, b], row_shift)
    xs = pick_each(xs, position)
    if number > 0:
        still = jnp.full((ROWS, 128), count) > number
        return [jnp.where(still, x, field[b]) for b, x in enumerate(xs)]
    return [x * sea for x in xs]


def step_kernel(
    spectra, tables, wet, wind, send, recv, growth, dissipation, substeps, coupling, courant, result,
    field, lhs, wide, chosen, placed_at, going, coming, packed, windy,
    columns, coarse, grown, damped, weights, back,
    weight_sem, swap_send, swap_recv, own_sem, send_sem, recv_sem, back_send, back_recv,
    plane_sem, all_sem, counted, count_sem,
):
    nest, me = lax.axis_index("nest"), lax.axis_index("bin")
    slot = lax.div(me, 4)
    y, z, x_me = lax.div(me, 32), lax.rem(slot, 8), lax.rem(me, 4)
    ys = [lax.rem(y + d, 4) for d in range(4)]
    zs = [lax.rem(z + d, 8) for d in range(8)]
    xs_at = [lax.rem(x_me + d, 4) for d in range(4)]

    def integrator(dy, dz):
        q = ys[dy] * 8 + zs[dz]
        return q, q * 4 + lax.rem(2 * nest + 32 - ys[dy] - zs[dz], 4)

    def peer(dy, dz, dx):
        return ys[dy] * 32 + zs[dz] * 4 + xs_at[dx]

    far = [0, 1, 2, 3, 4, 3, 2, 1]
    near = [0, 1, 2, 1]
    slots = sorted(
        [(dy, dz) for dy in range(4) for dz in range(8)], key=lambda d: -(near[d[0]] + far[d[1]])
    )[:-1]
    sources = sorted(
        [(dy, dz, dx) for dy in range(4) for dz in range(8) for dx in range(4)],
        key=lambda d: -(near[d[0]] + far[d[1]] + near[d[2]]),
    )[:-1]
    own_device = integrator(0, 0)[1]
    integrates = own_device == me

    def to(device):
        return {"bin": device}

    def forward(q, device):
        return pltpu.make_async_remote_copy(
            src_ref=packed.at[pl.ds(q * BINS, BINS)],
            dst_ref=columns.at[pl.ds(me * BINS, BINS)],
            send_sem=send_sem,
            recv_sem=recv_sem,
            device_id=to(device),
            device_id_type=pl.DeviceIdType.MESH,
        )

    def returning(s):
        return pltpu.make_async_remote_copy(
            src_ref=columns.at[pl.ds(s * BINS, BINS)],
            dst_ref=back.at[pl.ds(slot * BINS, BINS)],
            send_sem=back_send,
            recv_sem=back_recv,
            device_id=to(s),
            device_id_type=pl.DeviceIdType.MESH,
        )

    def several(count, ref, sent, received):
        rows = ref.at[pl.ds(0, count * BINS)]
        return pltpu.make_async_remote_copy(
            src_ref=rows,
            dst_ref=rows,
            send_sem=sent,
            recv_sem=received,
            device_id=to(lax.rem(me + 1, SOURCES)),
            device_id_type=pl.DeviceIdType.MESH,
        )

    def own_in():
        return pltpu.make_async_copy(
            packed.at[pl.ds(slot * BINS, BINS)], columns.at[pl.ds(me * BINS, BINS)], own_sem
        )

    def own_out():
        return pltpu.make_async_copy(
            columns.at[pl.ds(me * BINS, BINS)], back.at[pl.ds(slot * BINS, BINS)], own_sem
        )

    def swap(number):
        return pltpu.make_async_remote_copy(
            src_ref=going.at[number],
            dst_ref=coming.at[number],
            send_sem=swap_send.at[number],
            recv_sem=swap_recv.at[number],
            device_id={"nest": 1 - nest},
            device_id_type=pl.DeviceIdType.MESH,
        )

    def send_halves(number, start):
        def half(i, carry):
            gather_send(send, chosen, lhs, going.at[2 * number + i], i)
            if start:
                swap(2 * number + i).start()
            return carry

        lax.fori_loop(0, 2, half, 0)

    def receive_halves(number):
        for half in range(2):
            swap(2 * number + half).wait_recv()
        return receive(coming.at[2 * number : 2 * number + 2], recv, wide, placed_at)

    def signal(semaphore, device):
        pl.semaphore_signal(
            semaphore, inc=1, device_id=device, device_id_type=pl.DeviceIdType.MESH
        )

    line_x = [to(peer(0, 0, d)) for d in range(1, 4)]
    line_y = [to(peer(d, 0, 0)) for d in range(1, 4)]
    line_z = [to(peer(0, d, 0)) for d in range(1, 8)]
    barrier = pltpu.get_barrier_semaphore()
    for device in line_z + line_y + line_x + [{"nest": 1 - nest}]:
        signal(barrier, device)

    fetch = pltpu.make_async_copy(coupling, weights, weight_sem)
    fetch.start()
    fetch_count = pltpu.make_async_copy(substeps, counted, count_sem)
    fetch_count.start()

    wet_int = load_split(wet)
    sea = wet_int.astype(f32)
    for b in range(BINS):
        x = load_split(spectra, b) * sea
        field[b] = x
        stage_rows(b, x, lhs)
    chosen[...] = onehot(send[...] & (GX - 1))
    placed_at[...] = onehot(recv[...] & (GX - 1))
    send_halves(0, False)
    order, position, turn = grid_order(tables)
    back_lane, leave, in_lane, enter, windy[...] = packing(wet_int, load_split(wind))
    fetch_count.wait()
    count = counted[0]

    pl.semaphore_wait(barrier, 14)
    swap(0).start()
    swap(1).start()
    for device in line_y:
        signal(plane_sem, device)
    placed = receive_halves(0)
    for b, x in enumerate(substep(0, placed, field, courant, count, order, position, sea, turn)):
        field[b] = x
        stage_rows(b, x, lhs)
    send_halves(1, True)
    pl.semaphore_wait(plane_sem, 3)
    for device in line_z:
        signal(all_sem, device)
    for block in range(BINS):
        at = slice(block * 128, (block + 1) * 128)
        grown[at, :] = jnp.transpose(jnp.broadcast_to((SOURCE_DT * growth[at]).reshape(1, 128), (128, 128)))
        damped[at, :] = jnp.transpose(jnp.broadcast_to((SOURCE_DT * dissipation[at]).reshape(1, 128), (128, 128)))

    placed = receive_halves(1)
    xs = pack(substep(1, placed, field, courant, count, order, position, sea, turn), in_lane, enter)
    for b, x in enumerate(xs):
        packed[pl.ds(b, SLOTS, stride=BINS), :] = x[:SLOTS]

    pl.semaphore_wait(all_sem, 7)
    for offset in slots:
        forward(*integrator(*offset)).start()
    fetch.wait()

    @pl.when(jnp.logical_not(integrates))
    def _():
        forward(slot, own_device).start()

    @pl.when(integrates)
    def _():
        own_in().start()
        several(SOURCES - 1, columns, send_sem, recv_sem).wait_recv()
        own_in().wait()
        blown = windy[pl.ds(slot, 1), :]

        def step(i, carry):
            v = columns[...]
            coarse[...] = v.astype(bf16)
            linear = jnp.dot(weights[...], coarse[...], preferred_element_type=f32)
            rms = jnp.sqrt(jnp.sum(v * v, axis=0, keepdims=True) * (1.0 / K) + TINY)
            columns[...] = (v + (SOURCE_DT * linear + grown[...] * blown * v)) / (
                1.0 + damped[...] * rms
            )
            return carry

        lax.fori_loop(0, SRC, step, 0)
        for offset in sources:
            returning(peer(*offset)).start()
        own_out().start()
        own_out().wait()
        several(SLOTS - 1, back, back_send, back_recv).wait_recv()

    @pl.when(jnp.logical_not(integrates))
    def _():
        several(SLOTS, back, back_send, back_recv).wait_recv()

    xs = unpack(
        [back[pl.ds(b, SLOTS, stride=BINS), :] for b in range(BINS)], back_lane, leave
    )
    for b, x in enumerate(xs):
        for half in range(2):
            result[b, pl.ds(half, GY, stride=2), :] = x[half * GY : (half + 1) * GY]

    for number in range(2 * SUBSTEPS):
        swap(number).wait_send()

    @pl.when(integrates)
    def _():
        several(SLOTS - 1, packed, send_sem, recv_sem).wait_send()
        several(SOURCES - 1, columns, back_send, back_recv).wait_send()

    @pl.when(jnp.logical_not(integrates))
    def _():
        several(SLOTS, packed, send_sem, recv_sem).wait_send()


def local(
    spectra, courant, coupling, growth, dissipation, wind,
    neighbours, wet_mask, send_list, recv_list, substep_count,
):
    plane = (ROWS, 128)
    tables = neighbours.reshape(4, ROWS, 128).transpose(1, 0, 2).reshape(4 * ROWS, 128)
    vmem = pl.BlockSpec(memory_space=pltpu.VMEM)
    smem = pl.BlockSpec(memory_space=pltpu.SMEM)
    result = pl.pallas_call(
        step_kernel,
        out_shape=pltpu.VMEM((BINS, ROWS, 128), f32),
        in_specs=[vmem] * 8 + [pl.BlockSpec(memory_space=pl.ANY)] * 2 + [smem],
        out_specs=vmem,
        scratch_shapes=[
            pltpu.VMEM((BINS, ROWS, 128), f32),
            pltpu.VMEM((2 * BINS * GY, GX), bf16),
            pltpu.VMEM((2 * BINS * GY + GY, NB), bf16),
            pltpu.VMEM((GX, NB), bf16),
            pltpu.VMEM((GX, NB), bf16),
            pltpu.VMEM((2 * SUBSTEPS, BINS, HALF), f32),
            pltpu.VMEM((2 * SUBSTEPS, BINS, HALF), f32),
            pltpu.VMEM((SLOTS * BINS, 128), f32),
            pltpu.VMEM((SLOTS, 128), f32),
            pltpu.VMEM((K, 128), f32),
            pltpu.VMEM((K, 128), bf16),
            pltpu.VMEM((K, 128), f32),
            pltpu.VMEM((K, 128), f32),
            pltpu.VMEM((K, K), bf16),
            pltpu.VMEM((SLOTS * BINS, 128), f32),
            pltpu.SemaphoreType.DMA,
            pltpu.SemaphoreType.DMA((2 * SUBSTEPS,)),
            pltpu.SemaphoreType.DMA((2 * SUBSTEPS,)),
            pltpu.SemaphoreType.DMA,
            pltpu.SemaphoreType.DMA,
            pltpu.SemaphoreType.DMA,
            pltpu.SemaphoreType.DMA,
            pltpu.SemaphoreType.DMA,
            pltpu.SemaphoreType.REGULAR,
            pltpu.SemaphoreType.REGULAR,
            pltpu.SMEM((1,), i32),
            pltpu.SemaphoreType.DMA,
        ],
        compiler_params=pltpu.CompilerParams(collective_id=0, has_side_effects=True),
    )(
        spectra.reshape(BINS, ROWS, 128), tables, wet_mask.reshape(plane), wind.reshape(plane),
        send_list, recv_list, growth, dissipation,
        substep_count, coupling, courant,
    )
    result = jnp.where(wet_mask.reshape(plane)[None] == 1, result, 0.0)
    return result.reshape(1, BINS, ROWS * 128)


def solution(mesh):
    in_specs = (
        P("nest", "bin", None), P(None, "bin"), P(), P(), P(), P("nest", None),
        P("nest", None, None), P("nest", None), P("nest", None), P("nest", None), P("nest"),
    )
    return jax.shard_map(
        local, mesh=mesh, in_specs=in_specs, out_specs=P("nest", "bin", None), check_vma=False
    )
```
